128 devices in a mesh: segment: 4 (over x), tensor: 32 (over z, y, core).
Axes of the slice: x: 4, y: 4, z: 4, core: 2. Of those that a mesh axis runs over, the one named last changes fastest.
Arguments:
- hidden: bfloat16 [4, 2, 768, 3072], P('segment', None, 'tensor'), may hold values from -6 to 6
- gate_weight: bfloat16 [4, 3072, 16384], P('segment', None, 'tensor'), may hold values from -0.109375 to 0.109375
- up_weight: bfloat16 [4, 3072, 16384], P('segment', None, 'tensor'), may hold values from -0.109375 to 0.109375
- down_weight: bfloat16 [4, 16384, 3072], P('segment', 'tensor'), may hold values from -0.046875 to 0.046875
- block_rows: int32 [4, 2, 6, 128], P('segment'), may hold values from 0 to 768, as said below
- slot_gate: float32 [4, 2, 6, 128], P('segment'), may hold values from 0.1 to 1
Outputs:
- handed: bfloat16 [4, 2, 768, 3072], P('segment', None, 'tensor')
The draws below stay inside these ranges and needn't reach their ends.
Inputs may be any that keep to these rules, and one draw needn't show every extreme that they name: `block_rows`: each entry is a token row of its micro-batch or 768 for an empty slot. Within one list of 768 slots the named rows are distinct and ascending and the empty slots come last; a list holds from 307 to 768 live slots, and both ends occur in every draw.
All inputs are finite; a program needn't handle non-finite values.
Results may differ from the reference program's by a relative error of at most 0.0085.
Values may be sent and summed in bfloat16 or wider, within the bound.
A program may use at most 128 MiB of HBM per device.

```python
import jax
import jax.numpy as jnp
from jax import lax

D = 3072
FF_DEV = 512
FF = 16384
M = 768
MB = 2
BLOCK = 128
NB = 6
SLOTS = 768
N_SEGMENT = 4
N_TENSOR = 32


def draw_block_rows(key, part):
    list_count = N_SEGMENT * MB
    key_list = jax.random.split(key, list_count)
    lowest = 2 * SLOTS // 5

    def draw_one(sub_key, position):
        first_key, second_key = jax.random.split(sub_key)
        live_count = jax.random.randint(first_key, (), lowest, SLOTS + 1)
        live_count = jnp.where(position == 0, SLOTS, live_count)
        live_count = jnp.where(position == MB, lowest, live_count)
        shuffled = jax.random.permutation(second_key, M)[:SLOTS]
        slot_ids = jnp.arange(SLOTS)
        picked = jnp.where(slot_ids < live_count, shuffled, M)
        return jnp.sort(picked).astype(jnp.int32)
    all_lists = jax.vmap(draw_one)(key_list, jnp.arange(list_count))
    return all_lists.reshape(N_SEGMENT, MB, NB, BLOCK)


def level_of(own_key, extent, cuts, smallest, top_value):
    def one(axis_at, parts):
        heights = jax.random.uniform(jax.random.fold_in(jax.random.fold_in(own_key, 6), axis_at), (parts,), jnp.float32, smallest / len(cuts), top_value / len(cuts))
        return jnp.repeat(jnp.exp(heights), extent[axis_at] // parts).reshape((-1,) + (1,) * (len(extent) - axis_at - 1))

    factor_of = one(*cuts[0])
    for cut in cuts[1:]:
        factor_of = factor_of * one(*cut)
    return factor_of


def scatter_about(key, shape, scale, reach, shards=(), held_as=jnp.bfloat16):
    array = scale * jax.random.normal(key, shape, jnp.float32)
    if shards:
        array = array * level_of(key, shape, shards, -0.22, 0.18)
    return jnp.clip(array, -reach, reach).astype(held_as)


def setup_inputs(seed: int = 0) -> dict:
    seeds = jax.random.split(jax.random.key(seed), 7)
    hidden = scatter_about(seeds[0], (N_SEGMENT, MB, M, D), 1.0, 6.0, ((0, 4), (2, 32)))
    gate_weight = scatter_about(seeds[1], (N_SEGMENT, D, FF), D ** -0.5, 0.109375, ((0, 4), (2, 32)))
    up_weight = scatter_about(seeds[2], (N_SEGMENT, D, FF), D ** -0.5, 0.109375, ((0, 4), (2, 32)))
    down_weight = scatter_about(seeds[3], (N_SEGMENT, FF, D), FF ** -0.5, 0.046875, ((0, 4), (1, 32)))
    block_rows = draw_block_rows(jax.random.fold_in(seeds[6], 71), 0)
    slot_gate = jnp.clip(0.1 + 0.9 * jax.random.uniform(seeds[5], (N_SEGMENT, MB, NB, BLOCK), jnp.float32) ** level_of(seeds[5], (N_SEGMENT, MB, NB, BLOCK), ((0, 4),), -0.2, 0.2), 0.1, 1.0)
    return {"hidden": hidden, "gate_weight": gate_weight, "up_weight": up_weight, "down_weight": down_weight, "block_rows": block_rows, "slot_gate": slot_gate}


def expert_phase(inputs):
    hidden, gate_weight, up_weight, down_weight, block_rows, slot_gate = inputs
    outputs = []
    for micro_batch in range(MB):
        tokens_in = hidden[micro_batch]
        padded = jnp.concatenate([tokens_in, jnp.zeros((1, D), tokens_in.dtype)], axis=0)
        indices = block_rows[micro_batch].reshape(SLOTS).astype(jnp.int32)
        slot_in = padded[indices]
        gate_act = jnp.dot(slot_in, gate_weight, preferred_element_type=jnp.float32)
        up_act = jnp.dot(slot_in, up_weight, preferred_element_type=jnp.float32)
        hidden_act = (jax.nn.silu(gate_act) * up_act).astype(jnp.bfloat16)
        grouped_act = hidden_act.reshape(SLOTS, N_TENSOR, FF_DEV).astype(jnp.float32)
        grouped_down = down_weight.reshape(N_TENSOR, FF_DEV, D).astype(jnp.float32)
        partial_value = jnp.einsum("sgf,gfd->gsd", grouped_act, grouped_down)
        gate_column = slot_gate[micro_batch].reshape(1, SLOTS, 1)
        rounded = (partial_value * gate_column).astype(jnp.bfloat16)
        rounded = lax.optimization_barrier(rounded)
        summed = jnp.sum(rounded.astype(jnp.float32), axis=0)
        placed = jnp.zeros((M + 1, D), jnp.float32).at[indices].add(summed)[:M]
        outputs.append((tokens_in.astype(jnp.float32) + placed).astype(jnp.bfloat16))
    return jnp.stack(outputs)


def reference(hidden, gate_weight, up_weight, down_weight, block_rows, slot_gate):
    phase_out = lax.map(expert_phase, (hidden, gate_weight, up_weight, down_weight, block_rows, slot_gate))
    return jnp.roll(phase_out, 1, axis=0)
```

```python
import jax
import jax.numpy as jnp
from jax import lax
from jax.sharding import PartitionSpec as P


def from_behind(value, axis, steps):
    count = lax.axis_size(axis)
    pairs = [(source, (source + steps) % count) for source in range(count)]
    return lax.ppermute(value, axis, pairs)


def per_device(hidden, gate_weight, up_weight, down_weight, block_rows, slot_gate):
    batches, shard_rows, features = hidden.shape[1:]
    count = lax.axis_size("tensor")
    own = hidden[0].reshape(batches * shard_rows, features)
    gathered = lax.all_gather(own, "tensor", axis=0, tiled=True)
    token = jnp.arange(count * shard_rows)
    hit = block_rows[0].reshape(batches, 1, -1) == token[None, :, None]
    gates = jnp.sum(jnp.where(hit, slot_gate[0].reshape(batches, 1, -1), 0.0), axis=2)
    column = gates.reshape(batches, count, shard_rows).transpose(1, 0, 2).reshape(-1, 1)
    gate_act = jnp.dot(gathered, gate_weight[0], preferred_element_type=jnp.float32)
    up_act = jnp.dot(gathered, up_weight[0], preferred_element_type=jnp.float32)
    hidden_act = (jax.nn.silu(gate_act) * up_act).astype(jnp.bfloat16)
    part = jnp.dot(hidden_act, down_weight[0], preferred_element_type=jnp.float32) * column
    summed = lax.psum_scatter(part.astype(jnp.bfloat16), "tensor", scatter_dimension=0, tiled=True)
    updated = (own.astype(jnp.float32) + summed.astype(jnp.float32)).astype(jnp.bfloat16)
    return from_behind(updated.reshape(hidden.shape), "segment", 1)


def solution(mesh):
    return jax.shard_map(
        per_device,
        mesh=mesh,
        in_specs=(
            P("segment", None, "tensor", None),
            P("segment", None, "tensor"),
            P("segment", None, "tensor"),
            P("segment", "tensor", None),
            P("segment", None, None, None),
            P("segment", None, None, None),
        ),
        out_specs=P("segment", None, "tensor", None),
        check_vma=False,
    )
```

```python
import jax
import jax.numpy as jnp
from jax import lax
from jax.experimental import pallas as pl
from jax.experimental.pallas import tpu as pltpu
from jax.sharding import PartitionSpec as P

MESH = pl.DeviceIdType.MESH
SIDE = 4
COPIES = 96


def kernel(
    segments, batches,
    h_ref, wg_ref, wu_ref, wd_ref, rows_ref, gates_ref, out_ref,
    x, o, rp, ra, rb, ru, rv, fa, fb, fu, fv, fin, wg, wu, wd, act, gcol,
    local_sem, send_sem, recv_sem,
):
    f32, bf16 = jnp.float32, jnp.bfloat16
    rows, width = h_ref.shape
    shard = rows // batches
    half = width // 2
    group = SIDE * rows
    units = wg.shape[1]
    seg, me = lax.axis_index("segment"), lax.axis_index("tensor")
    core = lax.rem(me, 2)
    y = lax.rem(lax.div(me, 2), SIDE)
    z = lax.div(me, 2 * SIDE)

    def member(c, d, e):
        dy = d * (1 - c) + e * c
        dz = e * (1 - c) + d * c
        return (lax.rem(z + dz, SIDE) * SIDE + lax.rem(y + dy, SIDE)) * 2 + c

    first_up, first_down = (seg, member(core, 1, 0)), (seg, member(core, SIDE - 1, 0))
    second_up, second_down = (seg, member(core, 0, 1)), (seg, member(core, 0, SIDE - 1))
    partner = (seg, me + 1 - 2 * core)
    ahead = (lax.rem(seg + 1, segments), me)
    behind = (lax.rem(seg + segments - 1, segments), me)

    cols = (pl.ds(0, half), pl.ds(half, half))
    everything = pl.ds(0, width)

    def slot(ref, f, d, e, part=everything):
        return ref.at[pl.ds(((f * SIDE + d) * SIDE + e) * rows, rows), part]

    def line(ref, d, *part):
        return ref.at[(pl.ds(d * rows, rows), *part)]

    used = []

    def copy(src, dst, device):
        k = len(used)
        made = pltpu.make_async_remote_copy(
            src_ref=src, dst_ref=dst, send_sem=send_sem.at[k], recv_sem=recv_sem.at[k],
            device_id=device, device_id_type=MESH,
        )
        used.append(made)
        return made

    def start(*made):
        for one in made:
            one.start()

    def arrived(*made):
        for one in made:
            one.wait_recv()

    p1p = copy(slot(x, 0, 0, 0), slot(x, 0, 3, 0), first_up)
    p1m = copy(slot(x, 0, 0, 0), slot(x, 0, 1, 0), first_down)
    p2p = copy(slot(x, 0, 3, 0, cols[0]), slot(x, 0, 2, 0, cols[0]), first_up)
    p2m = copy(slot(x, 0, 1, 0, cols[1]), slot(x, 0, 2, 0, cols[1]), first_down)
    qap = [copy(slot(x, 0, d, 0), slot(x, 0, d, 3), second_up) for d in range(SIDE)]
    qam = [copy(slot(x, 0, d, 0), slot(x, 0, d, 1), second_down) for d in range(SIDE)]
    qbp = [copy(slot(x, 0, d, 3, cols[0]), slot(x, 0, d, 2, cols[0]), second_up) for d in range(SIDE)]
    qbm = [copy(slot(x, 0, d, 1, cols[1]), slot(x, 0, d, 2, cols[1]), second_down) for d in range(SIDE)]
    over = [[copy(slot(x, 0, d, e), slot(x, 1, d, e), partner) for e in range(SIDE)] for d in range(SIDE)]

    def band(ref, f, d, part):
        return ref.at[pl.ds((f * SIDE + d) * group, group), part]

    back = [[copy(band(o, 1, d, c), band(rp, 0, d, c), partner) for c in cols] for d in range(SIDE)]
    r1p = [copy(slot(o, 0, d, 2, cols[0]), line(ra, d), second_up) for d in range(SIDE)]
    r1m = [copy(slot(o, 0, d, 2, cols[1]), line(rb, d), second_down) for d in range(SIDE)]
    r2p = [[copy(slot(o, 0, d, 1, c), line(ru, d, c), second_up) for c in cols] for d in range(SIDE)]
    r2m = [[copy(slot(o, 0, d, 3, c), line(rv, d, c), second_down) for c in cols] for d in range(SIDE)]
    f1p = copy(slot(o, 0, 2, 0, cols[0]), fa, first_up)
    f1m = copy(slot(o, 0, 2, 0, cols[1]), fb, first_down)
    f2p = [copy(slot(o, 0, 1, 0, c), fu.at[:, c], first_up) for c in cols]
    f2m = [copy(slot(o, 0, 3, 0, c), fv.at[:, c], first_down) for c in cols]
    hand = [copy(fin.at[:, c], out_ref.at[:, c], ahead) for c in cols]

    own = pltpu.make_async_copy(h_ref, slot(x, 0, 0, 0), local_sem.at[0])
    own.start()
    loads = [
        pltpu.make_async_copy(src, dst, local_sem.at[1 + k])
        for k, (src, dst) in enumerate(((wg_ref, wg), (wu_ref, wu), (wd_ref, wd)))
    ]
    start(*loads)

    barrier = pltpu.get_barrier_semaphore()
    near = (first_up, first_down, second_up, second_down, partner, ahead, behind)
    for device in near:
        pl.semaphore_signal(barrier, inc=1, device_id=device, device_id_type=MESH)
    pl.semaphore_wait(barrier, len(near))
    own.wait()
    start(p1p, p1m, over[0][0])

    def gate_of(k, carry):
        f = lax.div(k, SIDE * SIDE)
        source = member(core + f - 2 * core * f, lax.rem(lax.div(k, SIDE), SIDE), lax.rem(k, SIDE))
        token = lax.broadcasted_iota(jnp.int32, (shard, 128), 0) + source * shard
        for b in range(batches):
            total = jnp.zeros((shard, 128), f32)
            for block in range(rows_ref.shape[0]):
                named = rows_ref[block, b : b + 1, :]
                total += jnp.where(token == named, gates_ref[block, b : b + 1, :], 0.0)
            at = pl.multiple_of(k * rows + b * shard, 8)
            gcol[pl.ds(at, shard), :] = jnp.broadcast_to(
                jnp.sum(total, axis=1, keepdims=True), (shard, 128)
            )
        return carry

    lax.fori_loop(0, 2 * SIDE * SIDE, gate_of, 0)

    arrived(p1p)
    start(p2p)
    arrived(p1m)
    start(p2m, qap[0], qam[0], over[3][0], over[1][0])
    arrived(p2p, p2m)
    start(qap[2], qam[2], over[2][0])
    arrived(qap[0])
    start(qbp[0], over[0][3])
    arrived(qam[0])
    start(qbm[0], over[0][1], qap[1], qam[1])
    arrived(qap[2])
    start(qbp[2], over[2][3])
    arrived(qam[2])
    start(qbm[2], over[2][1], qap[3], qam[3])
    arrived(qbp[0], qbm[0])
    start(over[0][2])
    for load in loads:
        load.wait()

    step = min(256, units)
    wide = min(512, half)

    def first(f, d, n):
        at = (f * SIDE + d) * group
        tokens = x[pl.ds(at, group), :]
        part = pl.ds(n * step, step)
        g = jnp.dot(tokens, wg[:, part], preferred_element_type=f32)
        u = jnp.dot(tokens, wu[:, part], preferred_element_type=f32)
        gate = gcol[pl.ds(at, group), :]
        gate = jnp.concatenate([gate] * (step // 128), axis=1)
        act[f, :, part] = (g / (1.0 + jnp.exp(-g)) * u * gate).astype(bf16)

    def second(f, d, h):
        at = (f * SIDE + d) * group
        for n in range(half // wide):
            part = pl.ds(h * half + n * wide, wide)
            term = jnp.dot(act[f], wd[:, part], preferred_element_type=f32)
            if f == 0:
                term = term + rp[pl.ds(d * group, group), part].astype(f32)
            o[pl.ds(at, group), part] = term.astype(bf16)

    def add(into, *terms):
        total = into[...].astype(f32)
        for term in terms:
            total = total + term[...].astype(f32)
        into[...] = total.astype(bf16)

    def relay(d):
        arrived(r1p[d])
        add(slot(o, 0, d, 1, cols[0]), line(ra, d))
        start(r2p[d][0])
        arrived(r1m[d])
        add(slot(o, 0, d, 3, cols[1]), line(rb, d))
        start(r2m[d][1])

    def settle(d, h):
        arrived(r2p[d][h], r2m[d][h])
        add(slot(o, 0, d, 0, cols[h]), line(ru, d, cols[h]), line(rv, d, cols[h]))

    def nothing():
        pass

    def block(d, hooks, send):
        run = lambda k: hooks.get(k, nothing)()
        arrived(*over[d])
        first(1, d, 0)
        run(0)
        for n in range(1, units // step):
            first(1, d, n)
        run(1)
        second(1, d, 0)
        start(back[d][0])
        run(2)
        second(1, d, 1)
        start(back[d][1])
        run(3)
        first(0, d, 0)
        run(4)
        for n in range(1, units // step):
            first(0, d, n)
        run(5)
        arrived(back[d][0])
        second(0, d, 0)
        if send:
            start(r1p[d], r2m[d][0])
        run(6)
        arrived(back[d][1])
        second(0, d, 1)
        if send:
            start(r1m[d], r2p[d][1])
        run(7)

    def pass_on(d):
        arrived(qap[d])
        start(qbp[d], over[d][3])
        arrived(qam[d])
        start(qbm[d], over[d][1])

    def complete(d):
        arrived(qbp[d], qbm[d])
        start(over[d][2])

    def two_away():
        settle(2, 0)
        settle(2, 1)
        start(f1p, f1m)

    block(0, {5: lambda: pass_on(1), 7: lambda: complete(2)}, False)
    block(2, {4: lambda: pass_on(3), 7: lambda: complete(1)}, True)
    block(1, {0: lambda: complete(3), 4: lambda: relay(2)}, True)
    block(3, {1: two_away, 4: lambda: relay(1)}, True)
    start(r1p[0], r2m[0][0], r1m[0], r2p[0][1])
    settle(1, 0)
    settle(1, 1)
    start(f2p[1])
    arrived(f1p)
    add(slot(o, 0, 1, 0, cols[0]), fa)
    start(f2p[0])
    relay(3)
    relay(0)
    settle(3, 0)
    start(f2m[0])
    settle(3, 1)
    arrived(f1m)
    add(slot(o, 0, 3, 0, cols[1]), fb)
    start(f2m[1])
    for h in (1, 0):
        c = cols[h]
        settle(0, h)
        arrived(f2p[h], f2m[h])
        fin[:, c] = (
            slot(o, 0, 0, 0, c)[...].astype(f32)
            + fu[:, c].astype(f32)
            + fv[:, c].astype(f32)
            + slot(x, 0, 0, 0, c)[...].astype(f32)
        ).astype(bf16)
        start(hand[h])
    arrived(*hand)
    for made in used:
        made.wait_send()


def per_device(hidden, gate_weight, up_weight, down_weight, block_rows, slot_gate):
    batches, shard, width = hidden.shape[1:]
    rows = batches * shard
    units = gate_weight.shape[2]
    segments = lax.axis_size("segment")
    bf16 = jnp.bfloat16
    anywhere, vmem = pl.BlockSpec(memory_space=pl.ANY), pl.BlockSpec(memory_space=pltpu.VMEM)

    def body(*refs):
        kernel(segments, batches, *refs)

    handed = pl.pallas_call(
        body,
        out_shape=jax.ShapeDtypeStruct((rows, width), bf16),
        in_specs=[anywhere] * 4 + [vmem] * 2,
        out_specs=anywhere,
        scratch_shapes=[
            pltpu.VMEM((32 * rows, width), bf16),
            pltpu.VMEM((32 * rows, width), bf16),
            pltpu.VMEM((16 * rows, width), bf16),
            pltpu.VMEM((4 * rows, width // 2), bf16),
            pltpu.VMEM((4 * rows, width // 2), bf16),
            pltpu.VMEM((4 * rows, width), bf16),
            pltpu.VMEM((4 * rows, width), bf16),
            pltpu.VMEM((rows, width // 2), bf16),
            pltpu.VMEM((rows, width // 2), bf16),
            pltpu.VMEM((rows, width), bf16),
            pltpu.VMEM((rows, width), bf16),
            pltpu.VMEM((rows, width), bf16),
            pltpu.VMEM((width, units), bf16),
            pltpu.VMEM((width, units), bf16),
            pltpu.VMEM((units, width), bf16),
            pltpu.VMEM((2, 4 * rows, units), bf16),
            pltpu.VMEM((32 * rows, 128), jnp.float32),
            pltpu.SemaphoreType.DMA((4,)),
            pltpu.SemaphoreType.DMA((COPIES,)),
            pltpu.SemaphoreType.DMA((COPIES,)),
        ],
        compiler_params=pltpu.CompilerParams(
            collective_id=0, has_side_effects=True, vmem_limit_bytes=60 * 1024 * 1024
        ),
    )(
        hidden.reshape(rows, width),
        gate_weight[0],
        up_weight[0],
        down_weight[0],
        block_rows[0].transpose(1, 0, 2),
        slot_gate[0].transpose(1, 0, 2),
    )
    return handed.reshape(hidden.shape)


def solution(mesh):
    return jax.shard_map(
        per_device,
        mesh=mesh,
        in_specs=(
            P("segment", None, "tensor", None),
            P("segment", None, "tensor"),
            P("segment", None, "tensor"),
            P("segment", "tensor", None),
            P("segment", None, None, None),
            P("segment", None, None, None),
        ),
        out_specs=P("segment", None, "tensor", None),
        check_vma=False,
    )
```

```python
import jax
import jax.numpy as jnp
from jax import lax
from jax.experimental import pallas as pl
from jax.experimental.pallas import tpu as pltpu
from jax.sharding import PartitionSpec as P

MESH = pl.DeviceIdType.MESH
SIDE = 4
COPIES = 128
UNITS = (
    ((0, 0), (1, 0), (2, 0), (3, 0)),
    ((0, 1), (0, 3), (0, 2), (2, 3)),
    ((2, 1), (1, 1), (1, 3), (2, 2)),
    ((1, 2), (3, 1), (3, 3), (3, 2)),
)
ORDER = (
    "A0", "P2", "Q0", "B0", "P3", "A2", "A1", "F000", "O0", "F001", "F100", "C0",
    "F101", "A3", "S100", "S101", "B2", "S000", "O2", "S001", "F010", "F110", "B1", "F111",
    "S110", "O1", "S111", "F011", "S010", "B3", "R00", "N00", "O3", "S011", "R01", "N01",
    "C2", "F020", "F021", "F120", "C1", "F121", "S120", "C3", "S121", "L00", "S020", "N10",
    "R20", "N20", "F130", "L01", "F131", "S021", "N11", "R21", "N21", "S130", "T00", "S131",
    "F030", "F031", "L20", "S030", "R10", "R30", "N30", "S031", "R11", "T01", "R31", "N31",
    "L21", "T20", "L10", "L30", "L11", "L31", "T21", "T10", "D10", "T30", "D30", "T11",
    "D11", "T31", "D31", "H0", "H1",
)


def kernel(
    segments, batches,
    h_ref, wg_ref, wu_ref, wd_ref, rows_ref, gates_ref, out_ref,
    x, o, rp, ra, rb, ru, rv, fa, fb, fu, fv, fin, wg, wu, wd, act, gcol,
    local_sem, send_sem, recv_sem,
):
    f32, bf16 = jnp.float32, jnp.bfloat16
    rows, width = h_ref.shape
    shard = rows // batches
    half = width // 2
    group = SIDE * rows
    units = wg.shape[1]
    seg, me = lax.axis_index("segment"), lax.axis_index("tensor")
    core = lax.rem(me, 2)
    y = lax.rem(lax.div(me, 2), SIDE)
    z = lax.div(me, 2 * SIDE)

    def member(c, d, e):
        dy = d * (1 - c) + e * c
        dz = e * (1 - c) + d * c
        return (lax.rem(z + dz, SIDE) * SIDE + lax.rem(y + dy, SIDE)) * 2 + c

    first_up, first_down = (seg, member(core, 1, 0)), (seg, member(core, SIDE - 1, 0))
    second_up, second_down = (seg, member(core, 0, 1)), (seg, member(core, 0, SIDE - 1))
    partner = (seg, me + 1 - 2 * core)
    ahead = (lax.rem(seg + 1, segments), me)
    behind = (lax.rem(seg + segments - 1, segments), me)

    quarter = half // 2
    cols = (pl.ds(0, half), pl.ds(half, half))
    parts = tuple(pl.ds(k * quarter, quarter) for k in range(4))
    place = {owner: k for k, owner in enumerate(sum(UNITS, ()))}

    def slot(ref, f, d, e, *part):
        return ref.at[(pl.ds((f * SIDE * SIDE + place[d, e]) * rows, rows), *part)]

    def line(ref, d, *part):
        return ref.at[(pl.ds(d * rows, rows), *part)]

    used = []

    def copy(src, dst, device):
        k = len(used)
        made = pltpu.make_async_remote_copy(
            src_ref=src, dst_ref=dst, send_sem=send_sem.at[k], recv_sem=recv_sem.at[k],
            device_id=device, device_id_type=MESH,
        )
        used.append(made)
        return made

    def start(*made):
        for one in made:
            one.start()

    def arrived(*made):
        for one in made:
            one.wait_recv()

    def both(source, above, below, up, down):
        return [
            (copy(slot(x, 0, *source, cols[k]), slot(x, 0, *above, cols[k]), up),
             copy(slot(x, 0, *source, cols[1 - k]), slot(x, 0, *below, cols[1 - k]), down))
            for k in range(2)
        ]

    def onward(above, below, target, up, down):
        return (
            copy(slot(x, 0, *above, cols[0]), slot(x, 0, *target, cols[0]), up),
            copy(slot(x, 0, *below, cols[1]), slot(x, 0, *target, cols[1]), down),
        )

    p1 = both((0, 0), (3, 0), (1, 0), first_up, first_down)
    p2 = onward((3, 0), (1, 0), (2, 0), first_up, first_down)
    qa = [both((d, 0), (d, 3), (d, 1), second_up, second_down) for d in range(SIDE)]
    qb = [onward((d, 3), (d, 1), (d, 2), second_up, second_down) for d in range(SIDE)]
    over = {owner: copy(slot(x, 0, *owner), slot(x, 1, *owner), partner) for owner in place}

    def band(f, unit):
        return pl.ds((f * SIDE + unit) * group, group)

    back = [[copy(o.at[band(1, k), c], rp.at[band(0, k), c], partner) for c in cols] for k in range(SIDE)]
    pairs = [(2 * c, 2 * c + 1) for c in range(2)]

    def relayed(source, above, below, up, down):
        return [
            (copy(source(parts[k]), above(parts[c]), up), copy(source(parts[m]), below(parts[c]), down))
            for c, (k, m) in enumerate(pairs)
        ]

    def final(above, below, into_up, into_down, up, down):
        return [
            ((copy(above(parts[m]), into_up(parts[m]), up), copy(below(parts[k]), into_down(parts[k]), down)),
             (copy(above(parts[k]), into_up(parts[k]), up), copy(below(parts[m]), into_down(parts[m]), down)))
            for k, m in pairs
        ]

    term = lambda d, e: lambda part: slot(o, 0, d, e, part)
    at = lambda ref, d: lambda part: line(ref, d, part)
    r1 = [relayed(term(d, 2), at(ra, d), at(rb, d), second_up, second_down) for d in range(SIDE)]
    r2 = [final(term(d, 1), term(d, 3), at(ru, d), at(rv, d), second_up, second_down) for d in range(SIDE)]
    f1 = relayed(term(2, 0), at(fa, 0), at(fb, 0), first_up, first_down)
    f2 = final(term(1, 0), term(3, 0), at(fu, 0), at(fv, 0), first_up, first_down)
    hand = [copy(fin.at[:, c], out_ref.at[:, c], ahead) for c in cols]

    own = pltpu.make_async_copy(h_ref, slot(x, 0, 0, 0), local_sem.at[0])
    own.start()
    loads = [
        pltpu.make_async_copy(src, dst, local_sem.at[1 + k])
        for k, (src, dst) in enumerate(((wg_ref, wg), (wu_ref, wu), (wd_ref, wd)))
    ]
    start(*loads)

    barrier = pltpu.get_barrier_semaphore()
    near = (first_up, first_down, second_up, second_down, partner, ahead, behind)
    for device in near:
        pl.semaphore_signal(barrier, inc=1, device_id=device, device_id_type=MESH)

    def gates_for(f):
        for (d, e), k in place.items():
            source = member(core + f - 2 * core * f, d, e)
            token = lax.broadcasted_iota(jnp.int32, (shard, 128), 0) + source * shard
            for b in range(batches):
                total = jnp.zeros((shard, 128), f32)
                for block in range(rows_ref.shape[0]):
                    named = rows_ref[block, b : b + 1, :]
                    total += jnp.where(token == named, gates_ref[block, b : b + 1, :], 0.0)
                at = (f * SIDE * SIDE + k) * rows + b * shard
                gcol[pl.ds(at, shard), :] = jnp.broadcast_to(
                    jnp.sum(total, axis=1, keepdims=True), (shard, 128)
                )

    gates_for(0)
    pl.semaphore_wait(barrier, len(near))
    own.wait()
    start(*p1[0], *p1[1], over[0, 0])
    gates_for(1)

    step = units // 2
    wide = min(512, half)

    def first(f, unit, n):
        part = pl.ds(n * step, step)
        tokens = x[band(f, unit), :]
        g = jnp.dot(tokens, wg[:, part], preferred_element_type=f32)
        u = jnp.dot(tokens, wu[:, part], preferred_element_type=f32)
        gate = jnp.concatenate([gcol[band(f, unit), :]] * (step // 128), axis=1)
        act[f, :, part] = (g / (1.0 + jnp.exp(-g)) * u * gate).astype(bf16)

    def second(f, unit, h):
        if f == 0:
            arrived(back[unit][h])
        for n in range(half // wide):
            part = pl.ds(h * half + n * wide, wide)
            value = jnp.dot(act[f], wd[:, part], preferred_element_type=f32)
            if f == 0:
                value = value + rp[band(0, unit), part].astype(f32)
            o[band(f, unit), part] = value.astype(bf16)
        if f == 1:
            start(back[unit][h])

    def add(into, *terms):
        total = into[...].astype(f32)
        for term in terms:
            total = total + term[...].astype(f32)
        into[...] = total.astype(bf16)

    def forward(came, made):
        for one, next_one in zip(came, made):
            arrived(one)
            start(next_one)

    def side_shards(came, d, *owners):
        for one, owner in zip(came, owners):
            arrived(one)
            start(over[owner])

    def far_shard(came, owner):
        arrived(*came)
        start(over[owner])

    def send_shard(d):
        if d == 0:
            for one in p1[0]:
                one.wait_send()
        start(*qa[d][0], *qa[d][1])

    def multiply(f, unit, n):
        while loads:
            loads.pop().wait()
        if f == 1 and n == 0:
            arrived(*(over[owner] for owner in UNITS[unit]))
        first(f, unit, n)

    def relay(d, c):
        k, m = pairs[c]
        arrived(r1[d][c][0])
        add(slot(o, 0, d, 1, parts[k]), line(ra, d, parts[c]))
        start(r2[d][c][1][0])
        arrived(r1[d][c][1])
        add(slot(o, 0, d, 3, parts[m]), line(rb, d, parts[c]))
        start(r2[d][c][1][1])

    def settle(d, c):
        arrived(*r2[d][c][0], *r2[d][c][1])
        add(slot(o, 0, d, 0, cols[c]), line(ru, d, cols[c]), line(rv, d, cols[c]))
        if d == 2:
            start(*f1[c])
        elif d:
            start(f2[c][0][d // 2])

    def last_relay(d, c):
        arrived(f1[c][d // 2])
        add(slot(o, 0, d, 0, parts[pairs[c][d // 2]]), line((fa, fb)[d // 2], 0, parts[c]))
        start(f2[c][1][d // 2])

    def hand_on(c):
        arrived(*f2[c][0], *f2[c][1])
        part = cols[c]
        fin[:, part] = (
            slot(o, 0, 0, 0, part)[...].astype(f32)
            + fu[:, part].astype(f32)
            + fv[:, part].astype(f32)
            + slot(x, 0, 0, 0, part)[...].astype(f32)
        ).astype(bf16)
        start(hand[c])

    table = {
        "A": send_shard,
        "B": lambda d: forward(qa[d][0], qb[d]),
        "O": lambda d: side_shards(qa[d][1], d, (d, 3), (d, 1)),
        "C": lambda d: far_shard(qb[d], (d, 2)),
        "F": multiply,
        "S": second,
        "R": lambda d, c: start(*r1[d][c]),
        "N": lambda d, c: start(*r2[d][c][0]),
        "L": relay,
        "T": settle,
        "D": last_relay,
        "H": hand_on,
        "P": lambda k: forward(p1[0], p2) if k == 2 else far_shard(p2, (2, 0)),
        "Q": lambda k: side_shards(p1[1], 0, (3, 0), (1, 0)),
    }
    for token in ORDER:
        table[token[0]](*(int(n) for n in token[1:]))
    arrived(*hand)
    for made in used:
        if all(made is not one for one in p1[0]):
            made.wait_send()


def per_device(hidden, gate_weight, up_weight, down_weight, block_rows, slot_gate):
    batches, shard, width = hidden.shape[1:]
    rows = batches * shard
    units = gate_weight.shape[2]
    segments = lax.axis_size("segment")
    bf16 = jnp.bfloat16
    anywhere, vmem = pl.BlockSpec(memory_space=pl.ANY), pl.BlockSpec(memory_space=pltpu.VMEM)

    def body(*refs):
        kernel(segments, batches, *refs)

    handed = pl.pallas_call(
        body,
        out_shape=pltpu.VMEM((rows, width), bf16),
        in_specs=[anywhere] * 4 + [vmem] * 2,
        out_specs=anywhere,
        scratch_shapes=[
            pltpu.VMEM((32 * rows, width), bf16),
            pltpu.VMEM((32 * rows, width), bf16),
            pltpu.VMEM((16 * rows, width), bf16),
            pltpu.VMEM((4 * rows, width // 2), bf16),
            pltpu.VMEM((4 * rows, width // 2), bf16),
            pltpu.VMEM((4 * rows, width), bf16),
            pltpu.VMEM((4 * rows, width), bf16),
            pltpu.VMEM((rows, width // 2), bf16),
            pltpu.VMEM((rows, width // 2), bf16),
            pltpu.VMEM((rows, width), bf16),
            pltpu.VMEM((rows, width), bf16),
            pltpu.VMEM((rows, width), bf16),
            pltpu.VMEM((width, units), bf16),
            pltpu.VMEM((width, units), bf16),
            pltpu.VMEM((units, width), bf16),
            pltpu.VMEM((2, 4 * rows, units), bf16),
            pltpu.VMEM((32 * rows, 128), jnp.float32),
            pltpu.SemaphoreType.DMA((4,)),
            pltpu.SemaphoreType.DMA((COPIES,)),
            pltpu.SemaphoreType.DMA((COPIES,)),
        ],
        compiler_params=pltpu.CompilerParams(
            collective_id=0, has_side_effects=True, vmem_limit_bytes=60 * 1024 * 1024
        ),
    )(
        hidden.reshape(rows, width),
        gate_weight[0],
        up_weight[0],
        down_weight[0],
        block_rows[0].transpose(1, 0, 2),
        slot_gate[0].transpose(1, 0, 2),
    )
    return handed.reshape(hidden.shape)


def solution(mesh):
    return jax.shard_map(
        per_device,
        mesh=mesh,
        in_specs=(
            P("segment", None, "tensor", None),
            P("segment", None, "tensor"),
            P("segment", None, "tensor"),
            P("segment", "tensor", None),
            P("segment", None, None, None),
            P("segment", None, None, None),
        ),
        out_specs=P("segment", None, "tensor", None),
        check_vma=False,
    )
```

```python
import jax
import jax.numpy as jnp
from jax import lax
from jax.experimental import pallas as pl
from jax.experimental.pallas import tpu as pltpu
from jax.sharding import PartitionSpec as P

MESH = pl.DeviceIdType.MESH
SIDE = 4
COPIES = 128
UNITS = (
    ((0, 0), (1, 0), (2, 0), (0, 2)),
    ((0, 1), (2, 1), (0, 3), (2, 3)),
    ((3, 0), (1, 1), (1, 3), (2, 2)),
    ((1, 2), (3, 1), (3, 3), (3, 2)),
)
ORDER = (
    "A0", "P2", "Q0", "B0", "P3", "A2", "O0", "A1", "C0", "F000", "F100", "B2",
    "S100", "S101", "O2", "A3", "B1", "S000", "O1", "S001", "F110", "C2", "S110", "S111",
    "R00", "F010", "B3", "F120", "O3", "R01", "S010", "C1", "N20", "S011", "S120", "N21",
    "N00", "L00", "S121", "F020", "C3", "N01", "L01", "S020", "R20", "S021", "F130", "R21",
    "N10", "S130", "N11", "S131", "T00", "F030", "T01", "L20", "L21", "S030", "R10", "S031",
    "R30", "N30", "T20", "T21", "R11", "L10", "L30", "R31", "N31", "L11", "T10", "D10",
    "T30", "D30", "L31", "T11", "D11", "T31", "D31", "H0", "H1",
)


def kernel(
    segments, batches,
    h_ref, wg_ref, wu_ref, wd_ref, rows_any, gates_any, out_ref,
    x, o, rp, ra, rb, ru, rv, fa, fb, fu, fv, fin, wg, wu, wd, act, gcol, rows_ref, gates_ref,
    local_sem, send_sem, recv_sem,
):
    f32, bf16 = jnp.float32, jnp.bfloat16
    rows, width = h_ref.shape
    shard = rows // batches
    half = width // 2
    group = SIDE * rows
    units = wg.shape[1]
    seg, me = lax.axis_index("segment"), lax.axis_index("tensor")
    core = lax.rem(me, 2)
    y = lax.rem(lax.div(me, 2), SIDE)
    z = lax.div(me, 2 * SIDE)

    def member(c, d, e):
        dy = d * (1 - c) + e * c
        dz = e * (1 - c) + d * c
        return (lax.rem(z + dz, SIDE) * SIDE + lax.rem(y + dy, SIDE)) * 2 + c

    first_up, first_down = (seg, member(core, 1, 0)), (seg, member(core, SIDE - 1, 0))
    second_up, second_down = (seg, member(core, 0, 1)), (seg, member(core, 0, SIDE - 1))
    partner = (seg, me + 1 - 2 * core)
    ahead = (lax.rem(seg + 1, segments), me)
    behind = (lax.rem(seg + segments - 1, segments), me)

    cols = (pl.ds(0, half), pl.ds(half, half))
    narrow = width // 4
    groups = (pl.ds(0, width - narrow), pl.ds(width - narrow, narrow))
    parts = tuple(
        pl.ds(g.start + k * (g.size // 2), g.size // 2) for g in groups for k in range(2)
    )
    lanes = (pl.ds(0, half - narrow // 2), pl.ds(half - narrow // 2, narrow // 2))
    place = {owner: k for k, owner in enumerate(sum(UNITS, ()))}

    def slot(ref, f, d, e, *part):
        return ref.at[(pl.ds((f * SIDE * SIDE + place[d, e]) * rows, rows), *part)]

    def line(ref, d, *part):
        return ref.at[(pl.ds(d * rows, rows), *part)]

    used = []

    def copy(src, dst, device):
        k = len(used)
        made = pltpu.make_async_remote_copy(
            src_ref=src, dst_ref=dst, send_sem=send_sem.at[k], recv_sem=recv_sem.at[k],
            device_id=device, device_id_type=MESH,
        )
        used.append(made)
        return made

    def start(*made):
        for one in made:
            one.start()

    def arrived(*made):
        for one in made:
            one.wait_recv()

    def both(source, above, below, up, down):
        return [
            (copy(slot(x, 0, *source, cols[k]), slot(x, 0, *above, cols[k]), up),
             copy(slot(x, 0, *source, cols[1 - k]), slot(x, 0, *below, cols[1 - k]), down))
            for k in range(2)
        ]

    def onward(above, below, target, up, down):
        return (
            copy(slot(x, 0, *above, cols[0]), slot(x, 0, *target, cols[0]), up),
            copy(slot(x, 0, *below, cols[1]), slot(x, 0, *target, cols[1]), down),
        )

    p1 = both((0, 0), (3, 0), (1, 0), first_up, first_down)
    p2 = onward((3, 0), (1, 0), (2, 0), first_up, first_down)
    qa = [both((d, 0), (d, 3), (d, 1), second_up, second_down) for d in range(SIDE)]
    qb = [onward((d, 3), (d, 1), (d, 2), second_up, second_down) for d in range(SIDE)]
    over = {owner: copy(slot(x, 0, *owner), slot(x, 1, *owner), partner) for owner in place}

    def band(f, unit):
        return pl.ds((f * SIDE + unit) * group, group)

    back = [[copy(o.at[band(1, k), c], rp.at[band(0, k), c], partner) for c in groups] for k in range(SIDE)]
    pairs = [(2 * c, 2 * c + 1) for c in range(2)]

    def relayed(source, above, below, up, down):
        return [
            (copy(source(parts[k]), above(lanes[c]), up), copy(source(parts[m]), below(lanes[c]), down))
            for c, (k, m) in enumerate(pairs)
        ]

    def final(above, below, into_up, into_down, up, down):
        return [
            ((copy(above(parts[m]), into_up(parts[m]), up), copy(below(parts[k]), into_down(parts[k]), down)),
             (copy(above(parts[k]), into_up(parts[k]), up), copy(below(parts[m]), into_down(parts[m]), down)))
            for k, m in pairs
        ]

    term = lambda d, e: lambda part: slot(o, 0, d, e, part)
    at = lambda ref, d: lambda part: line(ref, d, part)
    r1 = [relayed(term(d, 2), at(ra, d), at(rb, d), second_up, second_down) for d in range(SIDE)]
    r2 = [final(term(d, 1), term(d, 3), at(ru, d), at(rv, d), second_up, second_down) for d in range(SIDE)]
    f1 = relayed(term(2, 0), at(fa, 0), at(fb, 0), first_up, first_down)
    f2 = final(term(1, 0), term(3, 0), at(fu, 0), at(fv, 0), first_up, first_down)
    hand = [copy(fin.at[:, c], out_ref.at[:, c], ahead) for c in groups]

    barrier = pltpu.get_barrier_semaphore()
    near = (first_up, first_down, second_up, second_down, partner, ahead, behind)
    for device in near:
        pl.semaphore_signal(barrier, inc=1, device_id=device, device_id_type=MESH)
    own, *loads = [
        pltpu.make_async_copy(src, dst, local_sem.at[k])
        for k, (src, dst) in enumerate(
            (
                (h_ref, slot(x, 0, 0, 0)), (rows_any, rows_ref), (gates_any, gates_ref),
                (wg_ref, wg), (wu_ref, wu), (wd_ref, wd),
            )
        )
    ]
    start(own, *loads)
    for _ in range(2):
        loads.pop(0).wait()

    def gates_for(f):
        for (d, e), k in place.items():
            source = member(core + f - 2 * core * f, d, e)
            token = lax.broadcasted_iota(jnp.int32, (shard, 128), 0) + source * shard
            for b in range(batches):
                total = jnp.zeros((shard, 128), f32)
                for block in range(rows_ref.shape[0]):
                    named = rows_ref[block, b : b + 1, :]
                    total += jnp.where(token == named, gates_ref[block, b : b + 1, :], 0.0)
                at = (f * SIDE * SIDE + k) * rows + b * shard
                gcol[pl.ds(at, shard), :] = jnp.broadcast_to(
                    jnp.sum(total, axis=1, keepdims=True), (shard, 128)
                )

    gates_for(0)
    pl.semaphore_wait(barrier, len(near))
    own.wait()
    start(*p1[0], *p1[1], over[0, 0])
    gates_for(1)

    step = units // 2

    def first(f, unit, _):
        for n in range(2):
            part = pl.ds(n * step, step)
            tokens = x[band(f, unit), :]
            g = jnp.dot(tokens, wg[:, part], preferred_element_type=f32)
            u = jnp.dot(tokens, wu[:, part], preferred_element_type=f32)
            gate = jnp.concatenate([gcol[band(f, unit), :]] * (step // 128), axis=1)
            act[f, :, part] = (g / (1.0 + jnp.exp(-g)) * u * gate).astype(bf16)

    def second(f, unit, h):
        if f == 0:
            arrived(back[unit][h])
        for n in range(groups[h].size // narrow):
            part = pl.ds(groups[h].start + n * narrow, narrow)
            value = jnp.dot(act[f], wd[:, part], preferred_element_type=f32)
            if f == 0:
                value = value + rp[band(0, unit), part].astype(f32)
            o[band(f, unit), part] = value.astype(bf16)
        if f == 1:
            start(back[unit][h])

    def add(into, *terms):
        total = into[...].astype(f32)
        for term in terms:
            total = total + term[...].astype(f32)
        into[...] = total.astype(bf16)

    def forward(came, made):
        for one, next_one in zip(came, made):
            arrived(one)
            start(next_one)

    def side_shards(came, d, *owners):
        for one, owner in zip(came, owners):
            arrived(one)
            start(over[owner])

    def far_shard(came, owner):
        arrived(*came)
        start(over[owner])

    def send_shard(d):
        if d == 0:
            for one in p1[0]:
                one.wait_send()
        start(*qa[d][0], *qa[d][1])

    def multiply(f, unit, n):
        while loads:
            loads.pop().wait()
        if f == 1 and n == 0:
            arrived(*(over[owner] for owner in UNITS[unit]))
        first(f, unit, n)

    def relay(d, c):
        k, m = pairs[c]
        arrived(r1[d][c][0])
        add(slot(o, 0, d, 1, parts[k]), line(ra, d, lanes[c]))
        start(r2[d][c][1][0])
        arrived(r1[d][c][1])
        add(slot(o, 0, d, 3, parts[m]), line(rb, d, lanes[c]))
        start(r2[d][c][1][1])

    def settle(d, c):
        arrived(*r2[d][c][0], *r2[d][c][1])
        add(slot(o, 0, d, 0, groups[c]), line(ru, d, groups[c]), line(rv, d, groups[c]))
        if d == 2:
            start(*f1[c])
        elif d:
            start(f2[c][0][d // 2])

    def last_relay(d, c):
        arrived(f1[c][d // 2])
        add(slot(o, 0, d, 0, parts[pairs[c][d // 2]]), line((fa, fb)[d // 2], 0, lanes[c]))
        start(f2[c][1][d // 2])

    def hand_on(c):
        arrived(*f2[c][0], *f2[c][1])
        part = groups[c]
        fin[:, part] = (
            slot(o, 0, 0, 0, part)[...].astype(f32)
            + fu[:, part].astype(f32)
            + fv[:, part].astype(f32)
            + slot(x, 0, 0, 0, part)[...].astype(f32)
        ).astype(bf16)
        start(hand[c])

    table = {
        "A": send_shard,
        "B": lambda d: forward(qa[d][0], qb[d]),
        "O": lambda d: side_shards(qa[d][1], d, (d, 3), (d, 1)),
        "C": lambda d: far_shard(qb[d], (d, 2)),
        "F": multiply,
        "S": second,
        "R": lambda d, c: start(*r1[d][c]),
        "N": lambda d, c: start(*r2[d][c][0]),
        "L": relay,
        "T": settle,
        "D": last_relay,
        "H": hand_on,
        "P": lambda k: forward(p1[0], p2) if k == 2 else far_shard(p2, (2, 0)),
        "Q": lambda k: side_shards(p1[1], 0, (3, 0), (1, 0)),
    }
    for token in ORDER:
        table[token[0]](*(int(n) for n in token[1:]))
    for made in used:
        if all(made is not one for one in (*p1[0], *hand)):
            made.wait_send()
    arrived(*hand)
    for made in hand:
        made.wait_send()


def per_device(hidden, gate_weight, up_weight, down_weight, block_rows, slot_gate):
    batches, shard, width = hidden.shape[1:]
    rows = batches * shard
    units = gate_weight.shape[2]
    segments = lax.axis_size("segment")
    bf16 = jnp.bfloat16
    anywhere = pl.BlockSpec(memory_space=pl.ANY)
    tables = block_rows[0].transpose(1, 0, 2), slot_gate[0].transpose(1, 0, 2)

    def body(*refs):
        kernel(segments, batches, *refs)

    handed = pl.pallas_call(
        body,
        out_shape=pltpu.VMEM((rows, width), bf16),
        in_specs=[anywhere] * 6,
        out_specs=anywhere,
        scratch_shapes=[
            pltpu.VMEM((32 * rows, width), bf16),
            pltpu.VMEM((32 * rows, width), bf16),
            pltpu.VMEM((16 * rows, width), bf16),
            pltpu.VMEM((4 * rows, width // 2), bf16),
            pltpu.VMEM((4 * rows, width // 2), bf16),
            pltpu.VMEM((4 * rows, width), bf16),
            pltpu.VMEM((4 * rows, width), bf16),
            pltpu.VMEM((rows, width // 2), bf16),
            pltpu.VMEM((rows, width // 2), bf16),
            pltpu.VMEM((rows, width), bf16),
            pltpu.VMEM((rows, width), bf16),
            pltpu.VMEM((rows, width), bf16),
            pltpu.VMEM((width, units), bf16),
            pltpu.VMEM((width, units), bf16),
            pltpu.VMEM((units, width), bf16),
            pltpu.VMEM((2, 4 * rows, units), bf16),
            pltpu.VMEM((32 * rows, 128), jnp.float32),
            *(pltpu.VMEM(table.shape, table.dtype) for table in tables),
            pltpu.SemaphoreType.DMA((6,)),
            pltpu.SemaphoreType.DMA((COPIES,)),
            pltpu.SemaphoreType.DMA((COPIES,)),
        ],
        compiler_params=pltpu.CompilerParams(
            collective_id=0, has_side_effects=True, vmem_limit_bytes=60 * 1024 * 1024
        ),
    )(
        hidden.reshape(rows, width),
        gate_weight[0],
        up_weight[0],
        down_weight[0],
        *tables,
    )
    return handed.reshape(hidden.shape)


def solution(mesh):
    return jax.shard_map(
        per_device,
        mesh=mesh,
        in_specs=(
            P("segment", None, "tensor", None),
            P("segment", None, "tensor"),
            P("segment", None, "tensor"),
            P("segment", "tensor", None),
            P("segment", None, None, None),
            P("segment", None, None, None),
        ),
        out_specs=P("segment", None, "tensor", None),
        check_vma=False,
    )
```

```python
import math

import jax
import jax.numpy as jnp
from jax import lax
from jax.experimental import pallas as pl
from jax.experimental.pallas import tpu as pltpu
from jax.sharding import PartitionSpec as P

MESH = pl.DeviceIdType.MESH
SIDE = 4
SENDERS, RECEIVERS = 13, 63
UNITS = (
    ((1, 0), (0, 0), (3, 0)),
    ((0, 3), (0, 2), (0, 1)),
    ((1, 3), (1, 1), (2, 1)),
    ((2, 3), (1, 2), (2, 2)),
    ((3, 1), (3, 2), (2, 0), (3, 3)),
)
ORDER = (
    "A0", "P2", "B0", "Q0", "A1", "O0", "F100", "S100", "P3", "A2", "F000", "C0",
    "B1", "S101", "F110", "S111", "B2", "S110", "A3", "S000", "O1", "O2", "S001", "F010",
    "C1", "S011", "S010", "R00", "F120", "C2", "S121", "B3", "R01", "S120", "N00", "F130",
    "S131", "S130", "L00", "F020", "S021", "O3", "N01", "N11", "S020", "N10", "C3", "F030",
    "S031", "L01", "R11", "S030", "R20", "N20", "R21", "T00", "N21", "F140", "S141", "R10",
    "S140", "F040", "L20", "S041", "N31", "L21", "R31", "S040", "R30", "N30", "L11", "L10",
    "L31", "T21", "L30", "T01", "T11", "T20", "T31", "T10", "D31", "D11", "T30", "D10",
    "D30", "H1", "H0",
)


def kernel(
    segments, batches,
    h_ref, wg_ref, wu_ref, wd_ref, rows_any, gates_any, out_ref,
    x, o, rp, far, near_by, fa, fb, ends, fin, wg, wu, wd, act, gcol, rows_ref, gates_ref,
    local_sem, send_sem, recv_sem,
):
    f32, bf16 = jnp.float32, jnp.bfloat16
    rows, width = h_ref.shape
    shard = rows // batches
    half = width // 2
    units = wg.shape[1]
    seg, me = lax.axis_index("segment"), lax.axis_index("tensor")
    core = lax.rem(me, 2)
    y = lax.rem(lax.div(me, 2), SIDE)
    z = lax.div(me, 2 * SIDE)

    def member(c, d, e):
        dy = d * (1 - c) + e * c
        dz = e * (1 - c) + d * c
        return (lax.rem(z + dz, SIDE) * SIDE + lax.rem(y + dy, SIDE)) * 2 + c

    first_up, first_down = (seg, member(core, 1, 0)), (seg, member(core, SIDE - 1, 0))
    second_up, second_down = (seg, member(core, 0, 1)), (seg, member(core, 0, SIDE - 1))
    partner = (seg, me + 1 - 2 * core)
    ahead = (lax.rem(seg + 1, segments), me)
    behind = (lax.rem(seg + segments - 1, segments), me)

    cols = (pl.ds(0, half), pl.ds(half, half))
    narrow = width // 4
    groups = (pl.ds(0, width - narrow), pl.ds(width - narrow, narrow))
    parts = tuple(
        pl.ds(g.start + k * (g.size // 2), g.size // 2) for g in groups for k in range(2)
    )
    lanes = (pl.ds(0, half - narrow // 2), pl.ds(half - narrow // 2, narrow // 2))
    place = {owner: k for k, owner in enumerate(sum(UNITS, ()))}

    def slot(ref, f, d, e, *part):
        return ref.at[(pl.ds((f * SIDE * SIDE + place[d, e]) * rows, rows), *part)]

    def line(ref, d, *part):
        return ref.at[(pl.ds(d * rows, rows), *part)]

    senders, receivers, sent = {}, {}, {}

    def copy(src, dst, device, kind, *key):
        made = pltpu.make_async_remote_copy(
            src_ref=src, dst_ref=dst,
            send_sem=send_sem.at[senders.setdefault(kind, len(senders))],
            recv_sem=recv_sem.at[receivers.setdefault((kind, *key), len(receivers))],
            device_id=device, device_id_type=MESH,
        )
        sent.setdefault(kind, []).append(src.shape)
        return made

    def start(*made):
        for one in made:
            one.start()

    def arrived(whole, kind, *key):
        pltpu.make_async_remote_copy(
            src_ref=whole, dst_ref=whole, send_sem=send_sem.at[senders[kind]],
            recv_sem=recv_sem.at[receivers[kind, *key]], device_id=partner, device_id_type=MESH,
        ).wait_recv()

    def all_sent(kind):
        count = sum(math.prod(shape) for shape in sent[kind]) // width
        whole = x.at[pl.ds(0, count)]
        pltpu.make_async_remote_copy(
            src_ref=whole, dst_ref=whole, send_sem=send_sem.at[senders[kind]],
            recv_sem=recv_sem.at[0], device_id=partner, device_id_type=MESH,
        ).wait_send()

    def two(ref, d, *part):
        return ref.at[(pl.ds(2 * d * rows, 2 * rows), *part)]

    def shard_of(owner, *part):
        return slot(x, 0, *owner, *part) if any(owner) else h_ref.at[(slice(None), *part)]

    def both(source, above, below, up, down, kind, d):
        return [
            (copy(shard_of(source, cols[k]), slot(x, 0, *above, cols[k]), up, kind + str(k), d, 0),
             copy(shard_of(source, cols[1 - k]), slot(x, 0, *below, cols[1 - k]), down, kind + str(k), d, 1))
            for k in range(2)
        ]

    def onward(above, below, target, up, down, kind, d):
        return (
            copy(slot(x, 0, *above, cols[0]), slot(x, 0, *target, cols[0]), up, kind, d),
            copy(slot(x, 0, *below, cols[1]), slot(x, 0, *target, cols[1]), down, kind, d),
        )

    unit_of = {owner: k for k, unit in enumerate(UNITS) for owner in unit}
    p1 = both((0, 0), (3, 0), (1, 0), first_up, first_down, "p", 0)
    p2 = onward((3, 0), (1, 0), (2, 0), first_up, first_down, "p2", 0)
    qa = [both((d, 0), (d, 3), (d, 1), second_up, second_down, "q", d) for d in range(SIDE)]
    qb = [onward((d, 3), (d, 1), (d, 2), second_up, second_down, "q2", d) for d in range(SIDE)]
    over = {owner: copy(shard_of(owner), slot(x, 1, *owner), partner, "over", k) for owner, k in unit_of.items()}

    begin = [sum(len(unit) for unit in UNITS[:k]) for k in range(len(UNITS))]

    def band(f, unit):
        return pl.ds((f * SIDE * SIDE + begin[unit]) * rows, len(UNITS[unit]) * rows)

    back = [
        [copy(o.at[band(1, k), g], rp.at[band(0, k), g], partner, "back", k, c) for c, g in enumerate(groups)]
        for k in range(len(UNITS))
    ]
    pairs = [(2 * c, 2 * c + 1) for c in range(2)]

    def relayed(source, above, below, up, down, kind, d, apart):
        return [
            (copy(source(parts[k]), above(lanes[c]), up, kind, d, c),
             copy(source(parts[m]), below(lanes[c]), down, kind, d, c + 2 * apart))
            for c, (k, m) in enumerate(pairs)
        ]

    def final(above, below, into, d, up, down, kind):
        into_up, into_down = at(into, 2 * d), at(into, 2 * d + 1)
        return [
            ((copy(above(parts[m]), into_up(parts[m]), up, kind, d, c),
              copy(below(parts[k]), into_down(parts[k]), down, kind, d, c)),
             (copy(above(parts[k]), into_up(parts[k]), up, kind, d, c),
              copy(below(parts[m]), into_down(parts[m]), down, kind, d, c)))
            for c, (k, m) in enumerate(pairs)
        ]

    term = lambda d, e: lambda part: slot(o, 0, d, e, part)
    at = lambda ref, d: lambda part: line(ref, d, part)
    r1 = [
        relayed(term(d, 2), at(far, 2 * d), at(far, 2 * d + 1), second_up, second_down, "r1", d, 0)
        for d in range(SIDE)
    ]
    r2 = [final(term(d, 1), term(d, 3), near_by, d, second_up, second_down, "r2") for d in range(SIDE)]
    f1 = relayed(term(2, 0), at(fa, 0), at(fb, 0), first_up, first_down, "f1", 0, 1)
    f2 = final(term(1, 0), term(3, 0), ends, 0, first_up, first_down, "f2")
    hand = [copy(fin.at[:, g], out_ref.at[:, g], ahead, "hand") for g in groups]

    barrier = pltpu.get_barrier_semaphore()
    near = (first_up, first_down, second_up, second_down, partner, ahead, behind)
    for device in near:
        pl.semaphore_signal(barrier, inc=1, device_id=device, device_id_type=MESH)
    own, *loads = [
        pltpu.make_async_copy(src, dst, local_sem.at[k])
        for k, (src, dst) in enumerate(
            (
                (h_ref, slot(x, 0, 0, 0)), (rows_any, rows_ref), (gates_any, gates_ref),
                (wg_ref, wg), (wu_ref, wu), (wd_ref, wd),
            )
        )
    ]
    start(own, *loads)

    def gates_for(f):
        for (d, e), k in place.items():
            source = member(core + f - 2 * core * f, d, e)
            token = lax.broadcasted_iota(jnp.int32, (shard, 128), 0) + source * shard
            for b in range(batches):
                total = jnp.zeros((shard, 128), f32)
                for block in range(rows_ref.shape[0]):
                    named = rows_ref[block, b : b + 1, :]
                    total += jnp.where(token == named, gates_ref[block, b : b + 1, :], 0.0)
                at = (f * SIDE * SIDE + k) * rows + b * shard
                gcol[pl.ds(at, shard), :] = jnp.broadcast_to(
                    jnp.sum(total, axis=1, keepdims=True), (shard, 128)
                )

    pl.semaphore_wait(barrier, len(near))
    start(*p1[0], *p1[1], over[0, 0])
    for _ in range(2):
        loads.pop(0).wait()
    gates_for(0)
    gates_for(1)
    own.wait()

    step = units // 2

    def first(f, unit, _):
        for n in range(2):
            part = pl.ds(n * step, step)
            tokens = x[band(f, unit), :]
            g = jnp.dot(tokens, wg[:, part], preferred_element_type=f32)
            u = jnp.dot(tokens, wu[:, part], preferred_element_type=f32)
            gate = jnp.concatenate([gcol[band(f, unit), :]] * (step // 128), axis=1)
            act[f, : tokens.shape[0], part] = (g / (1.0 + jnp.exp(-g)) * u * gate).astype(bf16)

    def second(f, unit, h):
        if f == 0:
            arrived(rp.at[band(0, unit), groups[h]], "back", unit, h)
        for n in range(groups[h].size // narrow):
            part = pl.ds(groups[h].start + n * narrow, narrow)
            value = jnp.dot(act[f, : len(UNITS[unit]) * rows, :], wd[:, part], preferred_element_type=f32)
            if f == 0:
                value = value + rp[band(0, unit), part].astype(f32)
            o[band(f, unit), part] = value.astype(bf16)
        if f == 1:
            start(back[unit][h])

    def add(into, *terms):
        total = into[...].astype(f32)
        for term in terms:
            total = total + term[...].astype(f32)
        into[...] = total.astype(bf16)

    def forward(kind, d, made, *owners):
        for k, owner in enumerate(owners):
            arrived(slot(x, 0, *owner, cols[k]), kind, d, k)
            start(made[k])

    def side_shards(kind, d, *owners):
        for k, owner in enumerate(owners):
            arrived(slot(x, 0, *owner, cols[1 - k]), kind, d, k)
            start(over[owner])

    def far_shard(kind, d, owner):
        arrived(slot(x, 0, *owner), kind, d)
        start(over[owner])

    def send_shard(d):
        if d == 0:
            all_sent("p0")
        start(*qa[d][0], *qa[d][1])

    def multiply(f, unit, n):
        while loads:
            loads.pop().wait()
        if f == 1 and n == 0:
            arrived(x.at[band(1, unit)], "over", unit)
        first(f, unit, n)

    def relay(d, c):
        k, m = pairs[c]
        arrived(two(far, d, lanes[c]), "r1", d, c)
        add(slot(o, 0, d, 1, parts[k]), line(far, 2 * d, lanes[c]))
        start(r2[d][c][1][0])
        add(slot(o, 0, d, 3, parts[m]), line(far, 2 * d + 1, lanes[c]))
        start(r2[d][c][1][1])

    def settle(d, c):
        arrived(two(near_by, d, groups[c]), "r2", d, c)
        add(slot(o, 0, d, 0, groups[c]), line(near_by, 2 * d, groups[c]), line(near_by, 2 * d + 1, groups[c]))
        if d == 2:
            start(*f1[c])
        elif d:
            start(f2[c][0][d // 2])

    def last_relay(d, c):
        side = d // 2
        came = line((fa, fb)[side], 0, lanes[c])
        arrived(came, "f1", 0, c + 2 * side)
        add(slot(o, 0, d, 0, parts[pairs[c][side]]), came)
        start(f2[c][1][side])

    def hand_on(c):
        part = groups[c]
        arrived(two(ends, 0, part), "f2", 0, c)
        fin[:, part] = (
            slot(o, 0, 0, 0, part)[...].astype(f32)
            + line(ends, 0, part)[...].astype(f32)
            + line(ends, 1, part)[...].astype(f32)
            + slot(x, 0, 0, 0, part)[...].astype(f32)
        ).astype(bf16)
        start(hand[c])

    table = {
        "A": send_shard,
        "B": lambda d: forward("q0", d, qb[d], (d, 3), (d, 1)),
        "O": lambda d: side_shards("q1", d, (d, 3), (d, 1)),
        "C": lambda d: far_shard("q2", d, (d, 2)),
        "F": multiply,
        "S": second,
        "R": lambda d, c: start(*r1[d][c]),
        "N": lambda d, c: start(*r2[d][c][0]),
        "L": relay,
        "T": settle,
        "D": last_relay,
        "H": hand_on,
        "P": lambda k: forward("p0", 0, p2, (3, 0), (1, 0)) if k == 2 else far_shard("p2", 0, (2, 0)),
        "Q": lambda k: side_shards("p1", 0, (3, 0), (1, 0)),
    }
    for token in ORDER:
        table[token[0]](*(int(n) for n in token[1:]))
    for kind in sent:
        if kind not in ("p0", "hand"):
            all_sent(kind)
    arrived(out_ref, "hand")
    all_sent("hand")
    assert len(senders) <= SENDERS and len(receivers) <= RECEIVERS


def per_device(hidden, gate_weight, up_weight, down_weight, block_rows, slot_gate):
    batches, shard, width = hidden.shape[1:]
    rows = batches * shard
    units = gate_weight.shape[2]
    segments = lax.axis_size("segment")
    bf16 = jnp.bfloat16
    anywhere = pl.BlockSpec(memory_space=pl.ANY)
    tables = block_rows[0].transpose(1, 0, 2), slot_gate[0].transpose(1, 0, 2)

    def body(*refs):
        kernel(segments, batches, *refs)

    handed = pl.pallas_call(
        body,
        out_shape=pltpu.VMEM((rows, width), bf16),
        in_specs=[anywhere] * 6,
        out_specs=anywhere,
        scratch_shapes=[
            pltpu.VMEM((32 * rows, width), bf16),
            pltpu.VMEM((32 * rows, width), bf16),
            pltpu.VMEM((16 * rows, width), bf16),
            pltpu.VMEM((8 * rows, width // 2), bf16),
            pltpu.VMEM((8 * rows, width), bf16),
            pltpu.VMEM((rows, width // 2), bf16),
            pltpu.VMEM((rows, width // 2), bf16),
            pltpu.VMEM((2 * rows, width), bf16),
            pltpu.VMEM((rows, width), bf16),
            pltpu.VMEM((width, units), bf16),
            pltpu.VMEM((width, units), bf16),
            pltpu.VMEM((units, width), bf16),
            pltpu.VMEM((2, max(map(len, UNITS)) * rows, units), bf16),
            pltpu.VMEM((32 * rows, 128), jnp.float32),
            *(pltpu.VMEM(table.shape, table.dtype) for table in tables),
            pltpu.SemaphoreType.DMA((6,)),
            pltpu.SemaphoreType.DMA((SENDERS,)),
            pltpu.SemaphoreType.DMA((RECEIVERS,)),
        ],
        compiler_params=pltpu.CompilerParams(
            collective_id=0, has_side_effects=True, vmem_limit_bytes=60 * 1024 * 1024
        ),
    )(
        hidden.reshape(rows, width),
        gate_weight[0],
        up_weight[0],
        down_weight[0],
        *tables,
    )
    return handed.reshape(hidden.shape)


def solution(mesh):
    return jax.shard_map(
        per_device,
        mesh=mesh,
        in_specs=(
            P("segment", None, "tensor", None),
            P("segment", None, "tensor"),
            P("segment", None, "tensor"),
            P("segment", "tensor", None),
            P("segment", None, None, None),
            P("segment", None, None, None),
        ),
        out_specs=P("segment", None, "tensor", None),
        check_vma=False,
    )
```

```python
import math

import jax
import jax.numpy as jnp
from jax import lax
from jax.experimental import pallas as pl
from jax.experimental.pallas import tpu as pltpu
from jax.sharding import PartitionSpec as P

MESH = pl.DeviceIdType.MESH
SIDE = 4
SENDERS, RECEIVERS = 13, 63
NARROW = 0.5
UNITS = (
    ((0, 3), (0, 1), (3, 0)),
    ((1, 3), (1, 1), (0, 2)),
    ((2, 0), (2, 1), (2, 3)),
    ((0, 0), (1, 2), (2, 2)),
    ((3, 1), (3, 2), (1, 0), (3, 3)),
)
ORDER = (
    "A0", "P2", "B0", "Q0", "A1", "O0", "P3", "A2", "F100", "S100", "B1", "S101",
    "C0", "O1", "B2", "F000", "A3", "S001", "F110", "O2", "S110", "S111", "S000", "N01",
    "F010", "N00", "C1", "F120", "C2", "S120", "S121", "B3", "S011", "R01", "F130", "S010",
    "O3", "N10", "N11", "S130", "F020", "R00", "S131", "S021", "S020", "N21", "N20", "C3",
    "F030", "S030", "R10", "S031", "R21", "R11", "L00", "L01", "F140", "S141", "R20", "S140",
    "L21", "L10", "F040", "L11", "S041", "R31", "S040", "T01", "R30", "T21", "L20", "N31",
    "L31", "N30", "L30", "T20", "T11", "D11", "T10", "T31", "D31", "T00", "T30", "D30",
    "D10", "H1", "H0",
)


def kernel(
    segments, batches,
    h_ref, wg_ref, wu_ref, wd_ref, rows_any, gates_any, out_ref,
    x, o, rp, far, near_by, fa, fb, ends, fin, wg, wu, wd, act, gcol, rows_ref, gates_ref,
    local_sem, send_sem, recv_sem,
):
    f32, bf16 = jnp.float32, jnp.bfloat16
    rows, width = h_ref.shape
    shard = rows // batches
    half = width // 2
    units = wg.shape[1]
    seg, me = lax.axis_index("segment"), lax.axis_index("tensor")
    core = lax.rem(me, 2)
    y = lax.rem(lax.div(me, 2), SIDE)
    z = lax.div(me, 2 * SIDE)

    def member(c, d, e):
        dy = d * (1 - c) + e * c
        dz = e * (1 - c) + d * c
        return (lax.rem(z + dz, SIDE) * SIDE + lax.rem(y + dy, SIDE)) * 2 + c

    first_up, first_down = (seg, member(core, 1, 0)), (seg, member(core, SIDE - 1, 0))
    second_up, second_down = (seg, member(core, 0, 1)), (seg, member(core, 0, SIDE - 1))
    partner = (seg, me + 1 - 2 * core)
    ahead = (lax.rem(seg + 1, segments), me)
    behind = (lax.rem(seg + segments - 1, segments), me)

    cols = (pl.ds(0, half), pl.ds(half, half))
    narrow = int(width * NARROW)
    wide = min(narrow, 768)
    groups = (pl.ds(0, width - narrow), pl.ds(width - narrow, narrow))
    parts = tuple(
        pl.ds(g.start + k * (g.size // 2), g.size // 2) for g in groups for k in range(2)
    )
    lanes = (pl.ds(0, half - narrow // 2), pl.ds(half - narrow // 2, narrow // 2))
    place = {owner: k for k, owner in enumerate(sum(UNITS, ()))}

    def slot(ref, f, d, e, *part):
        return ref.at[(pl.ds((f * SIDE * SIDE + place[d, e]) * rows, rows), *part)]

    def line(ref, d, *part):
        return ref.at[(pl.ds(d * rows, rows), *part)]

    senders, receivers, sent = {}, {}, {}

    def copy(src, dst, device, kind, *key):
        made = pltpu.make_async_remote_copy(
            src_ref=src, dst_ref=dst,
            send_sem=send_sem.at[senders.setdefault(kind, len(senders))],
            recv_sem=recv_sem.at[receivers.setdefault((kind, *key), len(receivers))],
            device_id=device, device_id_type=MESH,
        )
        sent.setdefault(kind, []).append(src.shape)
        return made

    def start(*made):
        for one in made:
            one.start()

    def arrived(whole, kind, *key):
        pltpu.make_async_remote_copy(
            src_ref=whole, dst_ref=whole, send_sem=send_sem.at[senders[kind]],
            recv_sem=recv_sem.at[receivers[kind, *key]], device_id=partner, device_id_type=MESH,
        ).wait_recv()

    def all_sent(kind):
        count = sum(math.prod(shape) for shape in sent[kind]) // width
        whole = x.at[pl.ds(0, count)]
        pltpu.make_async_remote_copy(
            src_ref=whole, dst_ref=whole, send_sem=send_sem.at[senders[kind]],
            recv_sem=recv_sem.at[0], device_id=partner, device_id_type=MESH,
        ).wait_send()

    def two(ref, d, *part):
        return ref.at[(pl.ds(2 * d * rows, 2 * rows), *part)]

    def shard_of(owner, *part):
        return slot(x, 0, *owner, *part) if any(owner) else h_ref.at[(slice(None), *part)]

    def both(source, above, below, up, down, kind, d):
        return [
            (copy(shard_of(source, cols[k]), slot(x, 0, *above, cols[k]), up, kind + str(k), d, 0),
             copy(shard_of(source, cols[1 - k]), slot(x, 0, *below, cols[1 - k]), down, kind + str(k), d, 1))
            for k in range(2)
        ]

    def onward(above, below, target, up, down, kind, d):
        return (
            copy(slot(x, 0, *above, cols[0]), slot(x, 0, *target, cols[0]), up, kind, d),
            copy(slot(x, 0, *below, cols[1]), slot(x, 0, *target, cols[1]), down, kind, d),
        )

    unit_of = {owner: k for k, unit in enumerate(UNITS) for owner in unit}
    p1 = both((0, 0), (3, 0), (1, 0), first_up, first_down, "p", 0)
    p2 = onward((3, 0), (1, 0), (2, 0), first_up, first_down, "p2", 0)
    qa = [both((d, 0), (d, 3), (d, 1), second_up, second_down, "q", d) for d in range(SIDE)]
    qb = [onward((d, 3), (d, 1), (d, 2), second_up, second_down, "q2", d) for d in range(SIDE)]
    over = {owner: copy(shard_of(owner), slot(x, 1, *owner), partner, "over", k) for owner, k in unit_of.items()}

    begin = [sum(len(unit) for unit in UNITS[:k]) for k in range(len(UNITS))]

    def band(f, unit):
        return pl.ds((f * SIDE * SIDE + begin[unit]) * rows, len(UNITS[unit]) * rows)

    back = [
        [copy(o.at[band(1, k), g], rp.at[band(0, k), g], partner, "back", k, c) for c, g in enumerate(groups)]
        for k in range(len(UNITS))
    ]
    pairs = [(2 * c, 2 * c + 1) for c in range(2)]

    def relayed(source, above, below, up, down, kind, d, apart):
        return [
            (copy(source(parts[k]), above(lanes[c]), up, kind, d, c),
             copy(source(parts[m]), below(lanes[c]), down, kind, d, c + 2 * apart))
            for c, (k, m) in enumerate(pairs)
        ]

    def final(above, below, into, d, up, down, kind):
        into_up, into_down = at(into, 2 * d), at(into, 2 * d + 1)
        return [
            ((copy(above(parts[m]), into_up(parts[m]), up, kind, d, c),
              copy(below(parts[k]), into_down(parts[k]), down, kind, d, c)),
             (copy(above(parts[k]), into_up(parts[k]), up, kind, d, c),
              copy(below(parts[m]), into_down(parts[m]), down, kind, d, c)))
            for c, (k, m) in enumerate(pairs)
        ]

    term = lambda d, e: lambda part: slot(o, 0, d, e, part)
    at = lambda ref, d: lambda part: line(ref, d, part)
    r1 = [
        relayed(term(d, 2), at(far, 2 * d), at(far, 2 * d + 1), second_up, second_down, "r1", d, 0)
        for d in range(SIDE)
    ]
    r2 = [final(term(d, 1), term(d, 3), near_by, d, second_up, second_down, "r2") for d in range(SIDE)]
    f1 = relayed(term(2, 0), at(fa, 0), at(fb, 0), first_up, first_down, "f1", 0, 1)
    f2 = final(term(1, 0), term(3, 0), ends, 0, first_up, first_down, "f2")
    hand = [copy(fin.at[:, g], out_ref.at[:, g], ahead, "hand") for g in groups]

    barrier = pltpu.get_barrier_semaphore()
    near = (first_up, first_down, second_up, second_down, partner, ahead, behind)
    for device in near:
        pl.semaphore_signal(barrier, inc=1, device_id=device, device_id_type=MESH)
    own, *loads = [
        pltpu.make_async_copy(src, dst, local_sem.at[k])
        for k, (src, dst) in enumerate(
            (
                (h_ref, slot(x, 0, 0, 0)), (rows_any, rows_ref), (gates_any, gates_ref),
                (wg_ref, wg), (wu_ref, wu), (wd_ref, wd),
            )
        )
    ]
    start(own, *loads)

    def gates_for(f):
        for (d, e), k in place.items():
            source = member(core + f - 2 * core * f, d, e)
            token = lax.broadcasted_iota(jnp.int32, (shard, 128), 0) + source * shard
            for b in range(batches):
                total = jnp.zeros((shard, 128), f32)
                for block in range(rows_ref.shape[0]):
                    named = rows_ref[block, b : b + 1, :]
                    total += jnp.where(token == named, gates_ref[block, b : b + 1, :], 0.0)
                at = (f * SIDE * SIDE + k) * rows + b * shard
                gcol[pl.ds(at, shard), :] = jnp.broadcast_to(
                    jnp.sum(total, axis=1, keepdims=True), (shard, 128)
                )

    pl.semaphore_wait(barrier, len(near))
    start(*p1[0], *p1[1], over[0, 0])
    for _ in range(2):
        loads.pop(0).wait()
    gates_for(0)
    gates_for(1)
    own.wait()

    step = units // 2

    def first(f, unit, _):
        for n in range(2):
            part = pl.ds(n * step, step)
            tokens = x[band(f, unit), :]
            g = jnp.dot(tokens, wg[:, part], preferred_element_type=f32)
            u = jnp.dot(tokens, wu[:, part], preferred_element_type=f32)
            gate = jnp.concatenate([gcol[band(f, unit), :]] * (step // 128), axis=1)
            act[f, : tokens.shape[0], part] = (g / (1.0 + jnp.exp(-g)) * u * gate).astype(bf16)

    def second(f, unit, h):
        if f == 0:
            arrived(rp.at[band(0, unit), groups[h]], "back", unit, h)
        for n in range(groups[h].size // wide):
            part = pl.ds(groups[h].start + n * wide, wide)
            value = jnp.dot(act[f, : len(UNITS[unit]) * rows, :], wd[:, part], preferred_element_type=f32)
            if f == 0:
                value = value + rp[band(0, unit), part].astype(f32)
            o[band(f, unit), part] = value.astype(bf16)
        if f == 1:
            start(back[unit][h])

    def add(into, *terms):
        total = into[...].astype(f32)
        for term in terms:
            total = total + term[...].astype(f32)
        into[...] = total.astype(bf16)

    def forward(kind, d, made, *owners):
        for k, owner in enumerate(owners):
            arrived(slot(x, 0, *owner, cols[k]), kind, d, k)
            start(made[k])

    def side_shards(kind, d, *owners):
        for k, owner in enumerate(owners):
            arrived(slot(x, 0, *owner, cols[1 - k]), kind, d, k)
            start(over[owner])

    def far_shard(kind, d, owner):
        arrived(slot(x, 0, *owner), kind, d)
        start(over[owner])

    def send_shard(d):
        if d == 0:
            all_sent("p0")
        start(*qa[d][0], *qa[d][1])

    def multiply(f, unit, n):
        while loads:
            loads.pop().wait()
        if f == 1 and n == 0:
            arrived(x.at[band(1, unit)], "over", unit)
        first(f, unit, n)

    def relay(d, c):
        k, m = pairs[c]
        arrived(two(far, d, lanes[c]), "r1", d, c)
        add(slot(o, 0, d, 1, parts[k]), line(far, 2 * d, lanes[c]))
        start(r2[d][c][1][0])
        add(slot(o, 0, d, 3, parts[m]), line(far, 2 * d + 1, lanes[c]))
        start(r2[d][c][1][1])

    def settle(d, c):
        arrived(two(near_by, d, groups[c]), "r2", d, c)
        add(slot(o, 0, d, 0, groups[c]), line(near_by, 2 * d, groups[c]), line(near_by, 2 * d + 1, groups[c]))
        if d == 2:
            start(*f1[c])
        elif d:
            start(f2[c][0][d // 2])

    def last_relay(d, c):
        side = d // 2
        came = line((fa, fb)[side], 0, lanes[c])
        arrived(came, "f1", 0, c + 2 * side)
        add(slot(o, 0, d, 0, parts[pairs[c][side]]), came)
        start(f2[c][1][side])

    def hand_on(c):
        part = groups[c]
        arrived(two(ends, 0, part), "f2", 0, c)
        fin[:, part] = (
            slot(o, 0, 0, 0, part)[...].astype(f32)
            + line(ends, 0, part)[...].astype(f32)
            + line(ends, 1, part)[...].astype(f32)
            + slot(x, 0, 0, 0, part)[...].astype(f32)
        ).astype(bf16)
        start(hand[c])

    table = {
        "A": send_shard,
        "B": lambda d: forward("q0", d, qb[d], (d, 3), (d, 1)),
        "O": lambda d: side_shards("q1", d, (d, 3), (d, 1)),
        "C": lambda d: far_shard("q2", d, (d, 2)),
        "F": multiply,
        "S": second,
        "R": lambda d, c: start(*r1[d][c]),
        "N": lambda d, c: start(*r2[d][c][0]),
        "L": relay,
        "T": settle,
        "D": last_relay,
        "H": hand_on,
        "P": lambda k: forward("p0", 0, p2, (3, 0), (1, 0)) if k == 2 else far_shard("p2", 0, (2, 0)),
        "Q": lambda k: side_shards("p1", 0, (3, 0), (1, 0)),
    }
    for token in ORDER:
        table[token[0]](*(int(n) for n in token[1:]))
    for kind in sent:
        if kind not in ("p0", "hand"):
            all_sent(kind)
    arrived(out_ref, "hand")
    all_sent("hand")
    assert len(senders) <= SENDERS and len(receivers) <= RECEIVERS


def per_device(hidden, gate_weight, up_weight, down_weight, block_rows, slot_gate):
    batches, shard, width = hidden.shape[1:]
    rows = batches * shard
    units = gate_weight.shape[2]
    segments = lax.axis_size("segment")
    bf16 = jnp.bfloat16
    anywhere = pl.BlockSpec(memory_space=pl.ANY)
    tables = block_rows[0].transpose(1, 0, 2), slot_gate[0].transpose(1, 0, 2)

    def body(*refs):
        kernel(segments, batches, *refs)

    handed = pl.pallas_call(
        body,
        out_shape=pltpu.VMEM((rows, width), bf16),
        in_specs=[anywhere] * 6,
        out_specs=anywhere,
        scratch_shapes=[
            pltpu.VMEM((32 * rows, width), bf16),
            pltpu.VMEM((32 * rows, width), bf16),
            pltpu.VMEM((16 * rows, width), bf16),
            pltpu.VMEM((8 * rows, width // 2), bf16),
            pltpu.VMEM((8 * rows, width), bf16),
            pltpu.VMEM((rows, width // 2), bf16),
            pltpu.VMEM((rows, width // 2), bf16),
            pltpu.VMEM((2 * rows, width), bf16),
            pltpu.VMEM((rows, width), bf16),
            pltpu.VMEM((width, units), bf16),
            pltpu.VMEM((width, units), bf16),
            pltpu.VMEM((units, width), bf16),
            pltpu.VMEM((2, max(map(len, UNITS)) * rows, units), bf16),
            pltpu.VMEM((32 * rows, 128), jnp.float32),
            *(pltpu.VMEM(table.shape, table.dtype) for table in tables),
            pltpu.SemaphoreType.DMA((6,)),
            pltpu.SemaphoreType.DMA((SENDERS,)),
            pltpu.SemaphoreType.DMA((RECEIVERS,)),
        ],
        compiler_params=pltpu.CompilerParams(
            collective_id=0, has_side_effects=True, vmem_limit_bytes=60 * 1024 * 1024
        ),
    )(
        hidden.reshape(rows, width),
        gate_weight[0],
        up_weight[0],
        down_weight[0],
        *tables,
    )
    return handed.reshape(hidden.shape)


def solution(mesh):
    return jax.shard_map(
        per_device,
        mesh=mesh,
        in_specs=(
            P("segment", None, "tensor", None),
            P("segment", None, "tensor"),
            P("segment", None, "tensor"),
            P("segment", "tensor", None),
            P("segment", None, None, None),
            P("segment", None, None, None),
        ),
        out_specs=P("segment", None, "tensor", None),
        check_vma=False,
    )
```

```python
import math

import jax
import jax.numpy as jnp
from jax import lax
from jax.experimental import pallas as pl
from jax.experimental.pallas import tpu as pltpu
from jax.sharding import PartitionSpec as P

MESH = pl.DeviceIdType.MESH
SIDE = 4
SENDERS, RECEIVERS = 13, 63
NARROW = 0.5
UNITS = (
    ((0, 1), (1, 0), (3, 0)),
    ((0, 0), (0, 3), (0, 2)),
    ((1, 1), (2, 1), (1, 3)),
    ((2, 3), (1, 2), (2, 2)),
    ((3, 1), (3, 2), (2, 0), (3, 3)),
)
ORDER = (
    "A0", "P2", "B0", "Q0", "A1", "O0", "P3", "A2", "C0", "F100", "S101", "S100",
    "B1", "F110", "S110", "S111", "B2", "O1", "A3", "F000", "S001", "S000", "O2", "F010",
    "S011", "S010", "R01", "C1", "F120", "S120", "C2", "R00", "F020", "B3", "N01", "S121",
    "F130", "S131", "N00", "S020", "L01", "N10", "S130", "S021", "O3", "N11", "F030", "C3",
    "S031", "R21", "S030", "R11", "R10", "R20", "N21", "F140", "S141", "T01", "S140", "L00",
    "L21", "F040", "L11", "N20", "S041", "R31", "S040", "R30", "T21", "N31", "L20", "L31",
    "N30", "L30", "L10", "T00", "T20", "T11", "T31", "D31", "D11", "T10", "T30", "D10",
    "D30", "H1", "H0",
)


def kernel(
    segments, batches,
    h_ref, wg_ref, wu_ref, wd_ref, rows_any, gates_any, out_ref,
    x, o, rp, far, near_by, fa, fb, ends, fin, wg, wu, wd, act, gcol, rows_ref, gates_ref,
    local_sem, send_sem, recv_sem,
):
    f32, bf16 = jnp.float32, jnp.bfloat16
    rows, width = h_ref.shape
    shard = rows // batches
    half = width // 2
    units = wg.shape[1]
    seg, me = lax.axis_index("segment"), lax.axis_index("tensor")
    core = lax.rem(me, 2)
    y = lax.rem(lax.div(me, 2), SIDE)
    z = lax.div(me, 2 * SIDE)

    def member(c, d, e):
        dy = d * (1 - c) + e * c
        dz = e * (1 - c) + d * c
        return (lax.rem(z + dz, SIDE) * SIDE + lax.rem(y + dy, SIDE)) * 2 + c

    first_up, first_down = (seg, member(core, 1, 0)), (seg, member(core, SIDE - 1, 0))
    second_up, second_down = (seg, member(core, 0, 1)), (seg, member(core, 0, SIDE - 1))
    partner = (seg, me + 1 - 2 * core)
    ahead = (lax.rem(seg + 1, segments), me)
    behind = (lax.rem(seg + segments - 1, segments), me)

    cols = (pl.ds(0, half), pl.ds(half, half))
    narrow = int(width * NARROW)
    wide = min(narrow, 768)
    groups = (pl.ds(0, width - narrow), pl.ds(width - narrow, narrow))
    parts = tuple(
        pl.ds(g.start + k * (g.size // 2), g.size // 2) for g in groups for k in range(2)
    )
    lanes = (pl.ds(0, half - narrow // 2), pl.ds(half - narrow // 2, narrow // 2))
    place = {owner: k for k, owner in enumerate(sum(UNITS, ()))}

    def slot(ref, f, d, e, *part):
        return ref.at[(pl.ds((f * SIDE * SIDE + place[d, e]) * rows, rows), *part)]

    def line(ref, d, *part):
        return ref.at[(pl.ds(d * rows, rows), *part)]

    senders, receivers, sent = {}, {}, {}

    def copy(src, dst, device, kind, *key):
        made = pltpu.make_async_remote_copy(
            src_ref=src, dst_ref=dst,
            send_sem=send_sem.at[senders.setdefault(kind, len(senders))],
            recv_sem=recv_sem.at[receivers.setdefault((kind, *key), len(receivers))],
            device_id=device, device_id_type=MESH,
        )
        sent.setdefault(kind, []).append(src.shape)
        return made

    def start(*made):
        for one in made:
            one.start()

    def arrived(whole, kind, *key):
        pltpu.make_async_remote_copy(
            src_ref=whole, dst_ref=whole, send_sem=send_sem.at[senders[kind]],
            recv_sem=recv_sem.at[receivers[kind, *key]], device_id=partner, device_id_type=MESH,
        ).wait_recv()

    def all_sent(kind):
        count = sum(math.prod(shape) for shape in sent[kind]) // width
        whole = x.at[pl.ds(0, count)]
        pltpu.make_async_remote_copy(
            src_ref=whole, dst_ref=whole, send_sem=send_sem.at[senders[kind]],
            recv_sem=recv_sem.at[0], device_id=partner, device_id_type=MESH,
        ).wait_send()

    def two(ref, d, *part):
        return ref.at[(pl.ds(2 * d * rows, 2 * rows), *part)]

    def shard_of(owner, *part):
        return slot(x, 0, *owner, *part) if any(owner) else h_ref.at[(slice(None), *part)]

    def both(source, above, below, up, down, kind, d):
        return [
            (copy(shard_of(source, cols[k]), slot(x, 0, *above, cols[k]), up, kind + str(k), d, 0),
             copy(shard_of(source, cols[1 - k]), slot(x, 0, *below, cols[1 - k]), down, kind + str(k), d, 1))
            for k in range(2)
        ]

    def onward(above, below, target, up, down, kind, d):
        return (
            copy(slot(x, 0, *above, cols[0]), slot(x, 0, *target, cols[0]), up, kind, d),
            copy(slot(x, 0, *below, cols[1]), slot(x, 0, *target, cols[1]), down, kind, d),
        )

    unit_of = {owner: k for k, unit in enumerate(UNITS) for owner in unit}
    p1 = both((0, 0), (3, 0), (1, 0), first_up, first_down, "p", 0)
    p2 = onward((3, 0), (1, 0), (2, 0), first_up, first_down, "p2", 0)
    qa = [both((d, 0), (d, 3), (d, 1), second_up, second_down, "q", d) for d in range(SIDE)]
    qb = [onward((d, 3), (d, 1), (d, 2), second_up, second_down, "q2", d) for d in range(SIDE)]
    over = {owner: copy(shard_of(owner), slot(x, 1, *owner), partner, "over", k) for owner, k in unit_of.items()}

    begin = [sum(len(unit) for unit in UNITS[:k]) for k in range(len(UNITS))]

    def band(f, unit):
        return pl.ds((f * SIDE * SIDE + begin[unit]) * rows, len(UNITS[unit]) * rows)

    back = [
        [copy(o.at[band(1, k), g], rp.at[band(0, k), g], partner, "back", k, c) for c, g in enumerate(groups)]
        for k in range(len(UNITS))
    ]
    pairs = [(2 * c, 2 * c + 1) for c in range(2)]

    def relayed(source, above, below, up, down, kind, d, apart):
        return [
            (copy(source(parts[k]), above(lanes[c]), up, kind, d, c),
             copy(source(parts[m]), below(lanes[c]), down, kind, d, c + 2 * apart))
            for c, (k, m) in enumerate(pairs)
        ]

    def final(above, below, into, d, up, down, kind):
        into_up, into_down = at(into, 2 * d), at(into, 2 * d + 1)
        return [
            ((copy(above(parts[m]), into_up(parts[m]), up, kind, d, c),
              copy(below(parts[k]), into_down(parts[k]), down, kind, d, c)),
             (copy(above(parts[k]), into_up(parts[k]), up, kind, d, c),
              copy(below(parts[m]), into_down(parts[m]), down, kind, d, c)))
            for c, (k, m) in enumerate(pairs)
        ]

    term = lambda d, e: lambda part: slot(o, 0, d, e, part)
    at = lambda ref, d: lambda part: line(ref, d, part)
    r1 = [
        relayed(term(d, 2), at(far, 2 * d), at(far, 2 * d + 1), second_up, second_down, "r1", d, 0)
        for d in range(SIDE)
    ]
    r2 = [final(term(d, 1), term(d, 3), near_by, d, second_up, second_down, "r2") for d in range(SIDE)]
    f1 = relayed(term(2, 0), at(fa, 0), at(fb, 0), first_up, first_down, "f1", 0, 1)
    f2 = final(term(1, 0), term(3, 0), ends, 0, first_up, first_down, "f2")
    hand = [copy(fin.at[:, g], out_ref.at[:, g], ahead, "hand") for g in groups]

    barrier = pltpu.get_barrier_semaphore()
    near = (first_up, first_down, second_up, second_down, partner, ahead, behind)
    for device in near:
        pl.semaphore_signal(barrier, inc=1, device_id=device, device_id_type=MESH)
    own, *loads = [
        pltpu.make_async_copy(src, dst, local_sem.at[k])
        for k, (src, dst) in enumerate(
            (
                (h_ref, slot(x, 0, 0, 0)), (rows_any, rows_ref), (gates_any, gates_ref),
                (wg_ref, wg), (wu_ref, wu), (wd_ref, wd),
            )
        )
    ]
    start(own, *loads)

    def gates_for(f):
        for (d, e), k in place.items():
            source = member(core + f - 2 * core * f, d, e)
            token = lax.broadcasted_iota(jnp.int32, (shard, 128), 0) + source * shard
            for b in range(batches):
                total = jnp.zeros((shard, 128), f32)
                for block in range(rows_ref.shape[0]):
                    named = rows_ref[block, b : b + 1, :]
                    total += jnp.where(token == named, gates_ref[block, b : b + 1, :], 0.0)
                at = (f * SIDE * SIDE + k) * rows + b * shard
                gcol[pl.ds(at, shard), :] = jnp.broadcast_to(
                    jnp.sum(total, axis=1, keepdims=True), (shard, 128)
                )

    pl.semaphore_wait(barrier, len(near))
    start(*p1[0], *p1[1], over[0, 0])
    for _ in range(2):
        loads.pop(0).wait()
    gates_for(0)
    gates_for(1)
    own.wait()

    step = units // 2

    def first(f, unit, _):
        for n in range(2):
            part = pl.ds(n * step, step)
            tokens = x[band(f, unit), :]
            g = jnp.dot(tokens, wg[:, part], preferred_element_type=f32)
            u = jnp.dot(tokens, wu[:, part], preferred_element_type=f32)
            gate = jnp.concatenate([gcol[band(f, unit), :]] * (step // 128), axis=1)
            act[f, : tokens.shape[0], part] = (g / (1.0 + jnp.exp(-g)) * u * gate).astype(bf16)

    def second(f, unit, h):
        if f == 0:
            arrived(rp.at[band(0, unit), groups[h]], "back", unit, h)
        for n in range(groups[h].size // wide):
            part = pl.ds(groups[h].start + n * wide, wide)
            value = jnp.dot(act[f, : len(UNITS[unit]) * rows, :], wd[:, part], preferred_element_type=f32)
            if f == 0:
                value = value + rp[band(0, unit), part].astype(f32)
            o[band(f, unit), part] = value.astype(bf16)
        if f == 1:
            start(back[unit][h])

    def add(into, *terms):
        total = into[...].astype(f32)
        for term in terms:
            total = total + term[...].astype(f32)
        into[...] = total.astype(bf16)

    def forward(kind, d, made, *owners):
        for k, owner in enumerate(owners):
            arrived(slot(x, 0, *owner, cols[k]), kind, d, k)
            start(made[k])

    def side_shards(kind, d, *owners):
        for k, owner in enumerate(owners):
            arrived(slot(x, 0, *owner, cols[1 - k]), kind, d, k)
            start(over[owner])

    def far_shard(kind, d, owner):
        arrived(slot(x, 0, *owner), kind, d)
        start(over[owner])

    def send_shard(d):
        if d == 0:
            all_sent("p0")
        start(*qa[d][0], *qa[d][1])

    def multiply(f, unit, n):
        while loads:
            loads.pop().wait()
        if f == 1 and n == 0:
            arrived(x.at[band(1, unit)], "over", unit)
        first(f, unit, n)

    def relay(d, c):
        k, m = pairs[c]
        arrived(two(far, d, lanes[c]), "r1", d, c)
        add(slot(o, 0, d, 1, parts[k]), line(far, 2 * d, lanes[c]))
        start(r2[d][c][1][0])
        add(slot(o, 0, d, 3, parts[m]), line(far, 2 * d + 1, lanes[c]))
        start(r2[d][c][1][1])

    def settle(d, c):
        arrived(two(near_by, d, groups[c]), "r2", d, c)
        add(slot(o, 0, d, 0, groups[c]), line(near_by, 2 * d, groups[c]), line(near_by, 2 * d + 1, groups[c]))
        if d == 2:
            start(*f1[c])
        elif d:
            start(f2[c][0][d // 2])

    def last_relay(d, c):
        side = d // 2
        came = line((fa, fb)[side], 0, lanes[c])
        arrived(came, "f1", 0, c + 2 * side)
        add(slot(o, 0, d, 0, parts[pairs[c][side]]), came)
        start(f2[c][1][side])

    def hand_on(c):
        part = groups[c]
        arrived(two(ends, 0, part), "f2", 0, c)
        fin[:, part] = (
            slot(o, 0, 0, 0, part)[...].astype(f32)
            + line(ends, 0, part)[...].astype(f32)
            + line(ends, 1, part)[...].astype(f32)
            + slot(x, 0, 0, 0, part)[...].astype(f32)
        ).astype(bf16)
        start(hand[c])

    table = {
        "A": send_shard,
        "B": lambda d: forward("q0", d, qb[d], (d, 3), (d, 1)),
        "O": lambda d: side_shards("q1", d, (d, 3), (d, 1)),
        "C": lambda d: far_shard("q2", d, (d, 2)),
        "F": multiply,
        "S": second,
        "R": lambda d, c: start(*r1[d][c]),
        "N": lambda d, c: start(*r2[d][c][0]),
        "L": relay,
        "T": settle,
        "D": last_relay,
        "H": hand_on,
        "P": lambda k: forward("p0", 0, p2, (3, 0), (1, 0)) if k == 2 else far_shard("p2", 0, (2, 0)),
        "Q": lambda k: side_shards("p1", 0, (3, 0), (1, 0)),
    }
    for token in ORDER:
        table[token[0]](*(int(n) for n in token[1:]))
    for kind in sent:
        if kind not in ("p0", "hand"):
            all_sent(kind)
    arrived(out_ref, "hand")
    all_sent("hand")
    assert len(senders) <= SENDERS and len(receivers) <= RECEIVERS


def per_device(hidden, gate_weight, up_weight, down_weight, block_rows, slot_gate):
    batches, shard, width = hidden.shape[1:]
    rows = batches * shard
    units = gate_weight.shape[2]
    segments = lax.axis_size("segment")
    bf16 = jnp.bfloat16
    anywhere = pl.BlockSpec(memory_space=pl.ANY)
    tables = block_rows[0].transpose(1, 0, 2), slot_gate[0].transpose(1, 0, 2)

    def body(*refs):
        kernel(segments, batches, *refs)

    handed = pl.pallas_call(
        body,
        out_shape=pltpu.VMEM((rows, width), bf16),
        in_specs=[anywhere] * 6,
        out_specs=anywhere,
        scratch_shapes=[
            pltpu.VMEM((32 * rows, width), bf16),
            pltpu.VMEM((32 * rows, width), bf16),
            pltpu.VMEM((16 * rows, width), bf16),
            pltpu.VMEM((8 * rows, width // 2), bf16),
            pltpu.VMEM((8 * rows, width), bf16),
            pltpu.VMEM((rows, width // 2), bf16),
            pltpu.VMEM((rows, width // 2), bf16),
            pltpu.VMEM((2 * rows, width), bf16),
            pltpu.VMEM((rows, width), bf16),
            pltpu.VMEM((width, units), bf16),
            pltpu.VMEM((width, units), bf16),
            pltpu.VMEM((units, width), bf16),
            pltpu.VMEM((2, max(map(len, UNITS)) * rows, units), bf16),
            pltpu.VMEM((32 * rows, 128), jnp.float32),
            *(pltpu.VMEM(table.shape, table.dtype) for table in tables),
            pltpu.SemaphoreType.DMA((6,)),
            pltpu.SemaphoreType.DMA((SENDERS,)),
            pltpu.SemaphoreType.DMA((RECEIVERS,)),
        ],
        compiler_params=pltpu.CompilerParams(
            collective_id=0, has_side_effects=True, vmem_limit_bytes=60 * 1024 * 1024
        ),
    )(
        hidden.reshape(rows, width),
        gate_weight[0],
        up_weight[0],
        down_weight[0],
        *tables,
    )
    return handed.reshape(hidden.shape)


def solution(mesh):
    return jax.shard_map(
        per_device,
        mesh=mesh,
        in_specs=(
            P("segment", None, "tensor", None),
            P("segment", None, "tensor"),
            P("segment", None, "tensor"),
            P("segment", "tensor", None),
            P("segment", None, None, None),
            P("segment", None, None, None),
        ),
        out_specs=P("segment", None, "tensor", None),
        check_vma=False,
    )
```
